32 devices in a mesh: frames: 4 (over y, x), tiles: 8 (over z, core).
Axes of the slice: x: 2, y: 2, z: 4, core: 2. Of those that a mesh axis runs over, the one named last changes fastest.
Arguments:
- features: bfloat16 [16, 64, 480, 128], P('frames', 'tiles'), may hold values from -6 to 6
- w_conv: bfloat16 [3, 3, 128, 128], replicated, may hold values from -0.1875 to 0.1875
- query_feats: bfloat16 [4096, 128], P(('frames', 'tiles')), may hold values from -6 to 6
- offset_rows: int32 [16, 32], P('frames'), may hold values from 0 to 7
- offset_cols: int32 [16, 32], P('frames'), may hold values from 0 to 471
- owners: int32 [32, 1], replicated, may hold values from 0 to 7; in each aligned block of 32 rows (0 to 31, 32 to 63, ...) at most 12 rows name the same one
- start_frames: int32 [4096], P(('frames', 'tiles')), may hold values from 0 to 15
- w_corr: bfloat16 [81, 384], replicated, may hold values from -0.625 to 0.625
- w_feat: bfloat16 [128, 384], replicated, may hold values from -0.5 to 0.5
- time_embed: float32 [16, 384], replicated, may hold values from -3 to 3
- gain_attn: float32 [384], replicated, may hold values from 0.5 to 1.5
- w_qkv: bfloat16 [384, 1152], replicated, may hold values from -1.0716518 to 1.0716518
- w_attn_out: bfloat16 [384, 384], replicated, may hold values from -0.3125 to 0.3125
- gain_mlp: float32 [384], replicated, may hold values from 0.5 to 1.5
- w_up: bfloat16 [384, 1536], replicated, may hold values from -0.3125 to 0.3125
- w_down: bfloat16 [1536, 384], replicated, may hold values from -0.15625 to 0.15625
Outputs:
- refined: bfloat16 [4096, 16, 384], P(('frames', 'tiles'))
The draws below stay inside these ranges and needn't reach their ends.
Inputs may be any that keep to these rules, and one draw needn't show every extreme that they name: `owners`: no tile owns more than 12 query blocks; some tile owns exactly 12; every tile owns at least one.
All inputs are finite; a program needn't handle non-finite values.
Results may differ from the reference program's by a relative error of at most 0.0066.
Values may be sent and summed in bfloat16 or wider, within the bound.
A program may use at most 192 MiB of HBM per device.

```python
import math
import jax
import jax.numpy as jnp
import numpy as np
from jax import lax

C = 128
D = 384
HEADS = 8
MLP_UNITS = 1536
WIN = 9
QBLK = 128
WIDTH_COLS = 480
TILE_ROWS = 8
FRAMES = 16
HEIGHT = 64
BLOCKS = 32
TRACKS = 4096
CAP = 12
N_TILES = 8


def draw_w_qkv(key, part):
    base = jnp.clip(jax.random.normal(jax.random.fold_in(key, 11), (D, 3 * D), jnp.float32), -3.5, 3.5) * D ** (-0.5)
    return base.astype(jnp.bfloat16)


def with_ends(values, rng, smallest, top_value):
    shape = values.shape
    spot = [jax.random.randint(jax.random.fold_in(rng, axis), (), 0, shape[axis]) for axis in range(len(shape))]
    values = values.at[tuple(spot)].set(smallest)
    longest = shape.index(max(shape))
    spot[longest] = (spot[longest] + 1) % shape[longest]
    return values.at[tuple(spot)].set(top_value)


def block_scale(key, extent, split, low, high):
    loudness = 1.0
    for axis_at, shards_of in split:
        heights = jax.random.uniform(jax.random.fold_in(jax.random.fold_in(key, 6), axis_at), (shards_of,), jnp.float32, low / len(split), high / len(split))
        loudness = loudness * jnp.repeat(jnp.exp(heights), extent[axis_at] // shards_of).reshape((-1,) + (1,) * (len(extent) - 1 - axis_at))
    return loudness


def routed_block(stream_key, own, number, rows, count, top, limit, lean):
    order = jax.random.permutation(stream_key, count)
    packed, common = shares(count, rows * top, limit, lean, True), shares(count, rows * top, limit, lean, False)
    places = jnp.arange(count)

    def named(sizes, rotation):
        used = int((sizes > 0).sum())
        fixed = max(1, used // 4)
        moved = fixed + (places - fixed + rotation * (used - fixed)) % max(1, count - fixed)
        return jnp.zeros((count,), jnp.int32).at[order[jnp.where(places < fixed, places, moved)]].set(jnp.asarray(sizes, jnp.int32))

    sizes = jnp.where(number % 4 == 0, named(packed, number // 4), named(common, number - number // 4 - 1))
    mixed = jax.random.permutation(jax.random.fold_in(own, 3), count)
    giver, sink = mixed[0:count // 2 * 2:2], mixed[1:count // 2 * 2:2]
    slack = jnp.minimum(sizes[giver] - 1, limit - sizes[sink]) // 2
    slack = jnp.where((giver == order[0]) | (sink == order[0]) | (sizes[sink] == 0), 0, jnp.maximum(slack, 0))
    moved = jax.random.randint(jax.random.fold_in(own, 4), (count // 2,), 0, 1 << 20) % (slack + 1)
    sizes = sizes.at[giver].add(-moved).at[sink].add(moved)
    members = jnp.searchsorted(jnp.cumsum(sizes), jnp.arange(rows * top), side="right").astype(jnp.int32)
    listing = members.reshape(top, rows).T
    listing = listing[jax.random.permutation(jax.random.fold_in(own, 1), rows)]
    rotation = jax.random.randint(jax.random.fold_in(own, 2), (rows, 1), 0, top)
    return jnp.take_along_axis(listing, (jnp.arange(top)[None, :] + rotation) % top, axis=1)


def shares(count, total, limit, slope, full):
    portions = [(1 << 20) // math.isqrt(rank ** slope) + 1 for rank in range(1, count + 1)]
    largest = limit if full else min(limit, max(-(-total // count), total * portions[0] // sum(portions)))
    least = 1 if total - largest >= count - 1 else 0
    given, surplus = [largest] + [least] * (count - 1), total - largest - least * (count - 1)
    while surplus > 0:
        free = [i for i in range(1, count) if given[i] < largest] or [i for i in range(1, count) if given[i] < limit]
        whole, remaining = sum([portions[i] for i in free]), surplus
        for i in free:
            addition = min(limit - given[i], max(1, remaining * portions[i] // whole), surplus)
            given[i] = given[i] + addition
            surplus = surplus - addition
    return np.array(given)


def noise(rng, extent, spread, most, cuts=(), held_as=jnp.bfloat16):
    level = block_scale(rng, extent, cuts, -0.22, 0.18) if cuts else 1.0
    entries = jax.random.normal(rng, extent, jnp.float32) * spread * level
    return jnp.minimum(jnp.maximum(entries, -most), most).astype(held_as)


def setup_inputs(seed: int = 0) -> dict:
    key_of = jax.random.split(jax.random.key(seed), 17)
    features = noise(key_of[0], (FRAMES, HEIGHT, WIDTH_COLS, C), 1.0, 6.0, ((0, 4), (1, 8)))
    w_conv = noise(key_of[1], (3, 3, C, C), (9 * C) ** -0.5, 0.1875)
    query_feats = noise(key_of[2], (TRACKS, C), 1.0, 6.0, ((0, 32),))
    offset_rows = with_ends(jax.random.randint(key_of[3], (FRAMES, BLOCKS), 0, TILE_ROWS), jax.random.fold_in(key_of[3], 1), 0, TILE_ROWS - 1).astype(jnp.int32)
    offset_cols = with_ends(jax.random.randint(key_of[4], (FRAMES, BLOCKS), 0, WIDTH_COLS - WIN + 1), jax.random.fold_in(key_of[4], 1), 0, WIDTH_COLS - WIN).astype(jnp.int32)
    owners_keys = jax.random.split(jax.random.fold_in(key_of[5], 1), BLOCKS // BLOCKS)
    owners_turns = jax.random.permutation(jax.random.fold_in(key_of[5], 3), BLOCKS // BLOCKS)
    owners = jax.vmap(lambda own, number: routed_block(jax.random.fold_in(key_of[5], 2), own, number, BLOCKS, N_TILES, 1, CAP, 2))(owners_keys, owners_turns).reshape((BLOCKS, 1))
    start_frames = with_ends(jax.random.randint(key_of[6], (TRACKS,), 0, FRAMES), jax.random.fold_in(key_of[6], 1), 0, FRAMES - 1).astype(jnp.int32)
    w_corr = noise(key_of[7], (WIN * WIN, D), (WIN * WIN) ** -0.5, 0.625)
    w_feat = noise(key_of[8], (C, D), C ** -0.5, 0.5)
    time_embed = noise(key_of[9], (FRAMES, D), 0.5, 3.0, (), jnp.float32)
    gain_attn = jnp.clip(1.0 + 0.1 * jax.random.normal(key_of[10], (D,), jnp.float32), 0.5, 1.5)
    w_qkv = draw_w_qkv(jax.random.fold_in(key_of[16], 71), 0)
    w_attn_out = noise(key_of[12], (D, D), D ** -0.5, 0.3125)
    gain_mlp = jnp.clip(1.0 + 0.1 * jax.random.normal(key_of[13], (D,), jnp.float32), 0.5, 1.5)
    w_up = noise(key_of[14], (D, MLP_UNITS), D ** -0.5, 0.3125)
    w_down = noise(key_of[15], (MLP_UNITS, D), MLP_UNITS ** -0.5, 0.15625)
    return {"features": features, "w_conv": w_conv, "query_feats": query_feats, "offset_rows": offset_rows, "offset_cols": offset_cols, "owners": owners, "start_frames": start_frames, "w_corr": w_corr, "w_feat": w_feat, "time_embed": time_embed, "gain_attn": gain_attn, "w_qkv": w_qkv, "w_attn_out": w_attn_out, "gain_mlp": gain_mlp, "w_up": w_up, "w_down": w_down}


def conv_frame(frame, w_conv):
    rows, cols, chans = frame.shape
    padded = jnp.pad(frame, ((1, 1), (1, 1), (0, 0)))
    total = jnp.zeros((rows * cols, chans), jnp.float32)
    for a in range(3):
        for b in range(3):
            piece = padded[a:a + rows, b:b + cols].reshape(rows * cols, chans)
            total = total + jnp.dot(piece, w_conv[a, b], preferred_element_type=jnp.float32)
    return total.reshape(rows, cols, chans).astype(jnp.bfloat16)

def rms_scale(values, gain):
    return values * lax.rsqrt(lax.optimization_barrier(jnp.mean(values * values, axis=-1, keepdims=True)) + 1e-06) * gain

def token_layer(tokens, starts, gain_attn, w_qkv, w_attn_out, gain_mlp, w_up, w_down):
    tracks, frames, width = tokens.shape
    head = width // HEADS
    normed = rms_scale(tokens, gain_attn).astype(jnp.bfloat16)
    qkv = jnp.einsum('tfd,de->tfe', normed.astype(jnp.float32), w_qkv.astype(jnp.float32)).astype(jnp.bfloat16)
    query = qkv[..., :width].reshape(tracks, frames, HEADS, head).astype(jnp.float32)
    keys = qkv[..., width:2 * width].reshape(tracks, frames, HEADS, head).astype(jnp.float32)
    values = qkv[..., 2 * width:].reshape(tracks, frames, HEADS, head).astype(jnp.float32)
    scores = jnp.einsum('tfhe,tghe->thfg', query, keys) * head ** (-0.5)
    valid = jnp.arange(frames)[None, :] >= starts[:, None]
    scores = jnp.where(valid[:, None, None, :], scores, -1e+30)
    top = lax.optimization_barrier(jnp.max(scores, axis=-1, keepdims=True))
    weights = jnp.exp(scores - top)
    probs = (weights / lax.optimization_barrier(jnp.sum(weights, axis=-1, keepdims=True))).astype(jnp.bfloat16)
    attended = jnp.einsum('thfg,tghe->tfhe', probs.astype(jnp.float32), values).astype(jnp.bfloat16)
    attended = attended.reshape(tracks, frames, width)
    mixed = tokens + jnp.einsum('tfd,de->tfe', attended.astype(jnp.float32), w_attn_out.astype(jnp.float32))
    normed2 = rms_scale(mixed, gain_mlp).astype(jnp.bfloat16)
    hidden = jax.nn.gelu(jnp.einsum('tfd,de->tfe', normed2.astype(jnp.float32), w_up.astype(jnp.float32)), approximate=True).astype(jnp.bfloat16)
    result = mixed + jnp.einsum('tfe,ed->tfd', hidden.astype(jnp.float32), w_down.astype(jnp.float32))
    return result.astype(jnp.bfloat16)

def reference(features, w_conv, query_feats, offset_rows, offset_cols, owners, start_frames, w_corr, w_feat, time_embed, gain_attn, w_qkv, w_attn_out, gain_mlp, w_up, w_down):
    chans = features.shape[-1]
    conv = lax.map(lambda frame: conv_frame(frame, w_conv), features)
    padded = jnp.pad(conv, ((0, 0), (4, 4), (0, 0), (0, 0)))
    queries = query_feats.reshape(-1, QBLK, chans)

    def frame_patch(frame, row, col):
        zero_start = jnp.zeros((), jnp.int32)
        return lax.dynamic_slice(frame, (row.astype(jnp.int32), col.astype(jnp.int32), zero_start), (WIN, WIN, chans)).reshape(WIN * WIN, chans)

    def block_corr(inputs):
        query, rows, cols, owner = inputs
        base = (owner * TILE_ROWS).astype(jnp.int32)
        patches = jax.vmap(frame_patch)(padded, (base + rows).astype(jnp.int32), cols.astype(jnp.int32))
        corr = jnp.einsum('fkc,qc->fkq', patches.astype(jnp.float32), query.astype(jnp.float32)) * chans ** (-0.5)
        return corr.astype(jnp.bfloat16)
    corr_all = lax.map(block_corr, (queries, offset_rows.T, offset_cols.T, owners[:, 0]))
    starts = start_frames.reshape(-1, QBLK)

    def block_tokens(inputs):
        corr, query, start = inputs
        tokens = jnp.einsum('fkq,kd->qfd', corr.astype(jnp.float32), w_corr.astype(jnp.float32))
        tokens = tokens + jnp.dot(query, w_feat, preferred_element_type=jnp.float32)[:, None, :] + time_embed[None]
        return token_layer(tokens, start, gain_attn, w_qkv, w_attn_out, gain_mlp, w_up, w_down)
    refined = lax.map(block_tokens, (corr_all, queries, starts))
    return refined.reshape(-1, refined.shape[2], refined.shape[3])
```

```python
import functools
import math

import jax
import jax.numpy as jnp
from jax import lax
from jax.experimental import pallas as pl
from jax.experimental.pallas import tpu as pltpu
from jax.sharding import PartitionSpec as P

HEADS = 8
WIN = 9
QBLK = 128
CELLS = 88
REACH = WIN // 2
GROUP = 8
F32 = jnp.float32
BF16 = jnp.bfloat16
MESH = pl.DeviceIdType.MESH


def window_kernel(
    n_tiles, n_frames, owners, row_off, col_off, feat, w_conv, out, w_cat, padded, conv, win, parts, pairs, sums,
    lands, total, ready, feat_sem, pair_send, pair_recv, hop_send, hop_recv, out_send, out_recv,
):
    tile, group = lax.axis_index("tiles"), lax.axis_index("frames")
    frame_dev, rows, cols, chans = feat.shape
    blocks = owners.shape[0]
    per_group = blocks // n_frames
    blk_dev = out.shape[1]
    lots = n_frames * blk_dev
    area = WIN * WIN
    chips = n_tiles // 2
    chip, core = tile // 2, tile % 2
    first_half = 1 - (2 * chip) // chips
    near = (1 - first_half) * (chips - 1 - chip) + first_half * chip
    far = chips - 1 - near
    near_way, far_way = 1 - first_half, first_half

    def fetch(frame):
        return pltpu.make_async_copy(feat.at[frame], padded.at[frame, pl.ds(2, rows)], feat_sem.at[frame])

    for frame in range(frame_dev):
        fetch(frame).start()
    partner = (group, tile + 1 - 2 * core)
    sides = [(group, (tile + 2) % n_tiles), (group, (tile + n_tiles - 2) % n_tiles)]
    peers = [((group + step) % n_frames, tile) for step in range(1, n_frames)]
    barrier = pltpu.get_barrier_semaphore()
    for device in [partner] + sides + peers:
        pl.semaphore_signal(barrier, inc=1, device_id=device, device_id_type=MESH)

    blank = jnp.zeros((2, cols, chans), BF16)
    for frame in range(frame_dev):
        padded[frame, 0:2] = blank
        padded[frame, rows + 2 : rows + 4] = blank
    win[...] = jnp.zeros_like(win)
    total[...] = jnp.zeros_like(total)
    for y in range(WIN):
        conv[y] = jnp.zeros(conv.shape[1:], F32)
        conv[WIN + rows + 2 + y] = jnp.zeros(conv.shape[1:], F32)
    conv[WIN : WIN + rows + 2, cols:] = jnp.zeros((rows + 2, conv.shape[1] - cols, chans), F32)
    for a in range(3):
        for b in range(3):
            w_cat[a * chans : (a + 1) * chans, b * chans : (b + 1) * chans] = w_conv[a, b]

    def pairing(frame, dest):
        return pltpu.make_async_remote_copy(
            src_ref=parts.at[frame, 2 * dest + 1 - core],
            dst_ref=pairs.at[frame, dest],
            send_sem=pair_send.at[frame, dest],
            recv_sem=pair_recv.at[frame, dest],
            device_id=partner,
            device_id_type=MESH,
        )

    def hop(way, frame, dest):
        return pltpu.make_async_remote_copy(
            src_ref=sums.at[frame, dest],
            dst_ref=lands.at[way, frame, dest],
            send_sem=hop_send.at[frame, dest],
            recv_sem=hop_recv.at[way, frame, dest],
            device_id=(group, (tile + n_tiles + 2 - 4 * way) % n_tiles),
            device_id_type=MESH,
        )

    def handing(step, frame, giver):
        return pltpu.make_async_remote_copy(
            src_ref=ready.at[frame, pl.ds(peers[step][0] * blk_dev, blk_dev)],
            dst_ref=out.at[giver * frame_dev + frame],
            send_sem=out_send.at[step, frame],
            recv_sem=out_recv.at[step, frame],
            device_id=peers[step],
            device_id_type=MESH,
        )

    def convolve(frame):
        fetch(frame).wait()

        def conv_rows(pair, carry):
            for half in range(2):
                y = 2 * pair + half
                wide = jnp.concatenate([padded[frame, y], padded[frame, y + 1], padded[frame, y + 2]], axis=-1)
                sums_at = jnp.dot(wide, w_cat[...], preferred_element_type=F32)
                edge = jnp.zeros((1, chans), F32)
                left = jnp.concatenate([edge, sums_at[: cols - 1, :chans]], axis=0)
                right = jnp.concatenate([sums_at[1:, 2 * chans :], edge], axis=0)
                conv[WIN + y, :cols] = left + sums_at[:, chans : 2 * chans] + right
            return carry

        lax.fori_loop(0, (rows + 2) // 2, conv_rows, 0)

        @pl.when(tile == 0)
        def _():
            conv[WIN, :cols] = jnp.zeros((cols, chans), F32)

        @pl.when(tile == n_tiles - 1)
        def _():
            conv[WIN + rows + 1, :cols] = jnp.zeros((cols, chans), F32)

    def cut_all(frame):
        def cut(turn, carry):
            dest = (1 - first_half) * turn + first_half * (chips - 1 - turn)
            for side in range(2):
                slot = 2 * dest + side
                for group_at in range(n_frames):
                    for extra in range(blk_dev):
                        block = group_at * per_group + slot * blk_dev + extra
                        local = (owners[block] - tile) * rows + row_off[frame, block] - REACH
                        first = jnp.clip(local + 1, -WIN, rows + 2) + WIN
                        col = col_off[frame, block]
                        at = (group_at * blk_dev + extra) * area
                        for i in range(WIN):
                            win[side, at + i * WIN : at + (i + 1) * WIN, :] = conv[first + i, pl.ds(col, WIN), :]
                parts[frame, slot] = win[side].astype(BF16)
            pairing(frame, dest).start()
            return carry

        lax.fori_loop(0, chips, cut, 0)

    def own(frame, dest):
        pairing(frame, dest).wait_recv()
        return parts[frame, 2 * dest + core].astype(F32) + pairs[frame, dest].astype(F32)

    def move(way, frame):
        upstream = (1 - way) * chip + way * (chips - 1 - chip)

        def one(i, carry):
            dest = (1 - way) * (chips - 1 - i) + way * i
            mine = own(frame, dest)

            @pl.when(upstream > 0)
            def _():
                hop(way, frame, dest).wait_recv()
                sums[frame, dest] = (mine + lands[way, frame, dest].astype(F32)).astype(BF16)

            @pl.when(upstream == 0)
            def _():
                sums[frame, dest] = mine.astype(BF16)

            hop(way, frame, dest).start()
            return carry

        lax.fori_loop(0, chips - 1 - upstream, one, 0)

    def finish(frame):
        span = parts.shape[2]
        total[:span] = own(frame, chip)

        @pl.when(chip > 0)
        def _():
            hop(0, frame, chip).wait_recv()
            total[:span] = total[:span] + lands[0, frame, chip].astype(F32)

        @pl.when(chip < chips - 1)
        def _():
            hop(1, frame, chip).wait_recv()
            total[:span] = total[:span] + lands[1, frame, chip].astype(F32)

        for lot in range(lots):
            ready[frame, lot] = total[lot * area : lot * area + CELLS].astype(BF16)
        for step in range(n_frames - 1):
            handing(step, frame, group).start()
        out[group * frame_dev + frame] = ready[frame, pl.ds(group * blk_dev, blk_dev)]

    convolve(0)
    pl.semaphore_wait(barrier, 1 + len(sides) + len(peers))

    def advance(turn, carry):
        @pl.when((turn > 0) & (turn < frame_dev))
        def _():
            convolve(turn)

        @pl.when(turn < frame_dev)
        def _():
            cut_all(turn)

            @pl.when(near == 0)
            def _():
                move(near_way, turn)

        late = turn - far

        @pl.when((late >= 0) & (late < frame_dev))
        def _():
            finish(late)
            move(far_way, late)

        soon = turn - near

        @pl.when((near > 0) & (soon >= 0) & (soon < frame_dev))
        def _():
            move(near_way, soon)

        return carry

    lax.fori_loop(0, frame_dev + chips - 1, advance, 0)
    for frame in range(frame_dev):

        def drain(dest, carry):
            pairing(frame, dest).wait_send()

            @pl.when(dest != chip)
            def _():
                hop(0, frame, dest).wait_send()

            return carry

        lax.fori_loop(0, chips, drain, 0)
        for step in range(n_frames - 1):
            handing(step, frame, (group + n_frames - step - 1) % n_frames).wait()


def rms_scale(values, gain):
    return values * lax.rsqrt(jnp.mean(values * values, axis=-1, keepdims=True) + 1e-06) * gain


def token_kernel(
    bundle, patch, query, starts, w_corr, w_feat, time_embed, gain_attn, w_qkv, w_attn_out, gain_mlp,
    w_up, w_down, out, tokens, w_token, w_qkv_t,
):
    step = pl.program_id(0)
    frames, _, cells, chans = patch.shape
    width = w_feat.shape[1]
    head = width // HEADS
    span = GROUP * frames
    per_block = QBLK // (GROUP * bundle)

    @pl.when(step == 0)
    def _():
        w_token[:chans] = jnp.zeros((chans, width), BF16)
        w_token[: w_corr.shape[0]] = w_corr[...]
        w_token[chans:] = w_feat[...]
        w_qkv_t[...] = w_qkv[...].T

    @pl.when(step % per_block == 0)
    def _():
        queries = query[...]
        blank = jnp.zeros((chans - cells, chans), BF16)
        for some in range(0, frames, 4):
            corrs = []
            for frame in range(some, some + 4):
                window = jnp.concatenate([patch[frame, 0], blank], axis=0)
                corr = lax.dot_general(
                    queries, window, (((1,), (1,)), ((), ())), preferred_element_type=F32
                ) * chans ** (-0.5)
                corrs.append(jnp.concatenate([corr.astype(BF16), queries], axis=1))
            made = jnp.dot(jnp.concatenate(corrs, axis=0), w_token[...], preferred_element_type=F32)
            for n in range(4):
                tokens[some + n] = made[n * QBLK : (n + 1) * QBLK] + time_embed[some + n : some + n + 1, :]

    first = (step % per_block) * (GROUP * bundle)
    x = jnp.concatenate(
        [
            tokens[:, pl.ds(pl.multiple_of(first + GROUP * g, GROUP), GROUP), :].reshape(span, width)
            for g in range(bundle)
        ],
        axis=0,
    )
    normed = rms_scale(x, gain_attn[...]).astype(BF16)
    qkv = lax.dot_general(
        w_qkv_t[...], normed, (((1,), (1,)), ((), ())), preferred_element_type=F32
    ).astype(BF16)
    key_at = lax.broadcasted_iota(jnp.int32, (span, span), 0)
    query_at = lax.broadcasted_iota(jnp.int32, (span, span), 1)
    same = (key_at % GROUP) == (query_at % GROUP)
    power = head ** (-0.5) * math.log2(math.e)
    start_rows = jnp.broadcast_to(starts[...].astype(F32)[None, :], (GROUP, QBLK)).astype(BF16)
    source = lax.broadcasted_iota(jnp.int32, (QBLK, span), 0)
    track = lax.broadcasted_iota(jnp.int32, (QBLK, span), 1) % GROUP
    gathered = []
    for g in range(bundle):
        at = slice(g * span, (g + 1) * span)
        pick = (source == track + (first + GROUP * g)).astype(BF16)
        start = jnp.dot(start_rows, pick, preferred_element_type=F32)[:1].astype(jnp.int32)
        valid = same & ((key_at // GROUP) >= start)
        scores = [
            lax.dot_general(
                qkv[width + h * head : width + (h + 1) * head, at],
                qkv[h * head : (h + 1) * head, at],
                (((0,), (0,)), ((), ())),
                preferred_element_type=F32,
            )
            for h in range(HEADS)
        ]
        weights, totals = [], []
        for h in range(HEADS):
            score = jnp.where(valid, scores[h], -1e30)
            weight = jnp.exp2((score - jnp.max(score, axis=0, keepdims=True)) * power)
            totals.append(jnp.sum(weight, axis=0, keepdims=True))
            weights.append(weight.astype(BF16))
        heads = [
            jnp.dot(
                qkv[2 * width + h * head : 2 * width + (h + 1) * head, at],
                weights[h],
                preferred_element_type=F32,
            )
            for h in range(HEADS)
        ]
        gathered.append(
            jnp.concatenate([(heads[h] / totals[h]).astype(BF16) for h in range(HEADS)], axis=0)
        )
    attended = jnp.concatenate(gathered, axis=1)
    mixed = x + lax.dot_general(
        attended, w_attn_out[...], (((0,), (0,)), ((), ())), preferred_element_type=F32
    )
    normed2 = rms_scale(mixed, gain_mlp[...]).astype(BF16)
    hidden = jax.nn.gelu(
        jnp.dot(normed2, w_up[...], preferred_element_type=F32), approximate=True
    ).astype(BF16)
    result = mixed + jnp.dot(hidden, w_down[...], preferred_element_type=F32)
    result = result.astype(BF16)
    move = (query_at == (key_at % frames) * GROUP + key_at // frames).astype(BF16)
    for g in range(bundle):
        at = slice(g * span, (g + 1) * span)
        out[at, :] = jnp.dot(move, result[at, :], preferred_element_type=F32).astype(BF16)


def body(
    features, w_conv, query_feats, offset_rows, offset_cols, owners, start_frames, w_corr, w_feat,
    time_embed, gain_attn, w_qkv, w_attn_out, gain_mlp, w_up, w_down,
):
    n_tiles = lax.axis_size("tiles")
    n_frames = lax.axis_size("frames")
    frame_dev, rows, cols, chans = features.shape
    blocks = owners.shape[0]
    blk_dev = blocks // (n_frames * n_tiles)
    lots = n_frames * blk_dev
    frames_total = frame_dev * n_frames
    width = w_feat.shape[1]
    whole = pl.BlockSpec(memory_space=pltpu.VMEM)
    scalars = pl.BlockSpec(memory_space=pltpu.SMEM)

    chips = n_tiles // 2
    span_rows = -(-lots * WIN * WIN // 8) * 8
    total_rows = -(-((lots - 1) * WIN * WIN + CELLS) // 8) * 8
    patch = pl.pallas_call(
        functools.partial(window_kernel, n_tiles, n_frames),
        out_shape=jax.ShapeDtypeStruct((frames_total, blk_dev, CELLS, chans), BF16),
        in_specs=[scalars, scalars, scalars, pl.BlockSpec(memory_space=pl.ANY), whole],
        out_specs=whole,
        scratch_shapes=[
            pltpu.VMEM((3 * chans, 3 * chans), BF16),
            pltpu.VMEM((frame_dev, rows + 4, cols, chans), BF16),
            pltpu.VMEM((rows + 2 + 2 * WIN, cols + 16, chans), F32),
            pltpu.VMEM((2, span_rows, chans), F32),
            pltpu.VMEM((frame_dev, n_tiles, span_rows, chans), BF16),
            pltpu.VMEM((frame_dev, chips, span_rows, chans), BF16),
            pltpu.VMEM((frame_dev, chips, span_rows, chans), BF16),
            pltpu.VMEM((2, frame_dev, chips, span_rows, chans), BF16),
            pltpu.VMEM((total_rows, chans), F32),
            pltpu.VMEM((frame_dev, lots, CELLS, chans), BF16),
        ]
        + [pltpu.SemaphoreType.DMA((frame_dev,))]
        + [pltpu.SemaphoreType.DMA((frame_dev, chips))] * 3
        + [pltpu.SemaphoreType.DMA((2, frame_dev, chips))]
        + [pltpu.SemaphoreType.DMA((n_frames - 1, frame_dev))] * 2,
        compiler_params=pltpu.CompilerParams(collective_id=0, has_side_effects=True),
    )(owners[:, 0], offset_rows, offset_cols, features, w_conv)

    bundle = 4
    span = GROUP * frames_total
    tracks = blk_dev * QBLK
    per_block = QBLK // (GROUP * bundle)
    def fixed(shape):
        return pl.BlockSpec(shape, lambda s: (0,) * len(shape))

    refined = pl.pallas_call(
        functools.partial(token_kernel, bundle),
        grid=(tracks // (GROUP * bundle),),
        out_shape=jax.ShapeDtypeStruct((tracks * frames_total, width), BF16),
        in_specs=[
            pl.BlockSpec((frames_total, 1, CELLS, chans), lambda s: (0, s // per_block, 0, 0)),
            pl.BlockSpec((QBLK, chans), lambda s: (s // per_block, 0)),
            pl.BlockSpec((QBLK,), lambda s: (s // per_block,)),
            fixed(w_corr.shape),
            fixed(w_feat.shape),
            fixed(time_embed.shape),
            fixed((width,)),
            fixed(w_qkv.shape),
            fixed(w_attn_out.shape),
            fixed((width,)),
            fixed(w_up.shape),
            fixed(w_down.shape),
        ],
        out_specs=pl.BlockSpec((bundle * span, width), lambda s: (s, 0)),
        scratch_shapes=[
            pltpu.VMEM((frames_total, QBLK, width), F32),
            pltpu.VMEM((2 * chans, width), BF16),
            pltpu.VMEM((3 * width, width), BF16),
        ],
    )(
        patch, query_feats, start_frames, w_corr, w_feat, time_embed, gain_attn, w_qkv,
        w_attn_out, gain_mlp, w_up, w_down,
    )
    return refined.reshape(tracks, frames_total, width)


def solution(mesh):
    placed = (
        P("frames", "tiles", None, None),
        P(),
        P(("frames", "tiles"), None),
        P("frames", None),
        P("frames", None),
        P(),
        P(("frames", "tiles")),
    ) + (P(),) * 9
    return jax.shard_map(
        body,
        mesh=mesh,
        in_specs=placed,
        out_specs=P(("frames", "tiles"), None, None),
        check_vma=False,
    )
```

```python
import functools
import math

import jax
import jax.numpy as jnp
from jax import lax
from jax.experimental import pallas as pl
from jax.experimental.pallas import tpu as pltpu
from jax.sharding import PartitionSpec as P

HEADS = 8
WIN = 9
QBLK = 128
CELLS = 88
REACH = WIN // 2
GROUP = 8
F32 = jnp.float32
BF16 = jnp.bfloat16
MESH = pl.DeviceIdType.MESH


def window_kernel(
    n_tiles, n_frames, owners_in, row_in, col_in, feat, w_conv_in, out, owners, row_off, col_off, w_conv, w_cat, padded,
    conv, win, parts, pairs, sums, lands, total, ready, load_sem, feat_sem, pair_send, pair_recv, hop_send, hop_recv, out_send, out_recv,
):
    tile, group = lax.axis_index("tiles"), lax.axis_index("frames")
    frame_dev, rows, cols, chans = feat.shape
    blocks = owners.shape[0]
    per_group = blocks // n_frames
    blk_dev = out.shape[1]
    lots = n_frames * blk_dev
    area = WIN * WIN
    chips = n_tiles // 2
    chip, core = tile // 2, tile % 2
    first_half = 1 - (2 * chip) // chips
    near = (1 - first_half) * (chips - 1 - chip) + first_half * chip
    far = chips - 1 - near
    near_way, far_way = 1 - first_half, first_half

    def fetch(frame):
        return pltpu.make_async_copy(feat.at[frame], padded.at[frame, pl.ds(2, rows)], feat_sem.at[frame])

    loads = [
        pltpu.make_async_copy(source, target, load_sem.at[n])
        for n, (source, target) in enumerate(
            [(w_conv_in, w_conv), (owners_in, owners), (row_in, row_off), (col_in, col_off)]
        )
    ]
    fetch(0).start()
    for load in loads:
        load.start()
    for frame in range(1, frame_dev):
        fetch(frame).start()
    partner = (group, tile + 1 - 2 * core)
    sides = [(group, (tile + 2) % n_tiles), (group, (tile + n_tiles - 2) % n_tiles)]
    peers = [((group + step) % n_frames, tile) for step in range(1, n_frames)]
    barrier = pltpu.get_barrier_semaphore()
    for device in [partner] + sides + peers:
        pl.semaphore_signal(barrier, inc=1, device_id=device, device_id_type=MESH)

    blank = jnp.zeros((2, cols, chans), BF16)
    for frame in range(frame_dev):
        padded[frame, 0:2] = blank
        padded[frame, rows + 2 : rows + 4] = blank
    win[...] = jnp.zeros_like(win)
    total[...] = jnp.zeros_like(total)
    for y in range(WIN):
        conv[y] = jnp.zeros(conv.shape[1:], F32)
        conv[WIN + rows + 2 + y] = jnp.zeros(conv.shape[1:], F32)
    conv[WIN : WIN + rows + 2, cols:] = jnp.zeros((rows + 2, conv.shape[1] - cols, chans), F32)
    for load in loads:
        load.wait()
    for a in range(3):
        for b in range(3):
            w_cat[a * chans : (a + 1) * chans, b * chans : (b + 1) * chans] = w_conv[a, b]

    def pairing(frame, dest):
        return pltpu.make_async_remote_copy(
            src_ref=parts.at[frame, 2 * dest + 1 - core],
            dst_ref=pairs.at[frame, dest],
            send_sem=pair_send.at[frame, dest],
            recv_sem=pair_recv.at[frame, dest],
            device_id=partner,
            device_id_type=MESH,
        )

    def hop(way, frame, dest):
        return pltpu.make_async_remote_copy(
            src_ref=sums.at[frame, dest],
            dst_ref=lands.at[way, frame, dest],
            send_sem=hop_send.at[frame, dest],
            recv_sem=hop_recv.at[way, frame, dest],
            device_id=(group, (tile + n_tiles + 2 - 4 * way) % n_tiles),
            device_id_type=MESH,
        )

    def handing(step, frame, giver):
        return pltpu.make_async_remote_copy(
            src_ref=ready.at[frame, pl.ds(peers[step][0] * blk_dev, blk_dev)],
            dst_ref=out.at[giver * frame_dev + frame],
            send_sem=out_send.at[step, frame],
            recv_sem=out_recv.at[step, frame],
            device_id=peers[step],
            device_id_type=MESH,
        )

    def convolve(frame):
        fetch(frame).wait()

        def conv_rows(pair, carry):
            for half in range(2):
                y = 2 * pair + half
                wide = jnp.concatenate([padded[frame, y], padded[frame, y + 1], padded[frame, y + 2]], axis=-1)
                sums_at = jnp.dot(wide, w_cat[...], preferred_element_type=F32)
                edge = jnp.zeros((1, chans), F32)
                left = jnp.concatenate([edge, sums_at[: cols - 1, :chans]], axis=0)
                right = jnp.concatenate([sums_at[1:, 2 * chans :], edge], axis=0)
                conv[WIN + y, :cols] = left + sums_at[:, chans : 2 * chans] + right
            return carry

        lax.fori_loop(0, (rows + 2) // 2, conv_rows, 0)

        @pl.when(tile == 0)
        def _():
            conv[WIN, :cols] = jnp.zeros((cols, chans), F32)

        @pl.when(tile == n_tiles - 1)
        def _():
            conv[WIN + rows + 1, :cols] = jnp.zeros((cols, chans), F32)

    def cut_all(frame):
        def cut(turn, carry):
            dest = (1 - first_half) * turn + first_half * (chips - 1 - turn)
            for side in range(2):
                slot = 2 * dest + side
                for group_at in range(n_frames):
                    for extra in range(blk_dev):
                        block = group_at * per_group + slot * blk_dev + extra
                        local = (owners[block] - tile) * rows + row_off[frame, block] - REACH
                        first = jnp.clip(local + 1, -WIN, rows + 2) + WIN
                        col = col_off[frame, block]
                        at = (group_at * blk_dev + extra) * area
                        for i in range(WIN):
                            win[side, at + i * WIN : at + (i + 1) * WIN, :] = conv[first + i, pl.ds(col, WIN), :]
                parts[frame, slot] = win[side].astype(BF16)
            pairing(frame, dest).start()
            return carry

        lax.fori_loop(0, chips, cut, 0)

    def own(frame, dest):
        pairing(frame, dest).wait_recv()
        return parts[frame, 2 * dest + core].astype(F32) + pairs[frame, dest].astype(F32)

    def move(way, frame):
        upstream = (1 - way) * chip + way * (chips - 1 - chip)

        def one(i, carry):
            dest = (1 - way) * (chips - 1 - i) + way * i
            mine = own(frame, dest)

            @pl.when(upstream > 0)
            def _():
                hop(way, frame, dest).wait_recv()
                sums[frame, dest] = (mine + lands[way, frame, dest].astype(F32)).astype(BF16)

            @pl.when(upstream == 0)
            def _():
                sums[frame, dest] = mine.astype(BF16)

            hop(way, frame, dest).start()
            return carry

        lax.fori_loop(0, chips - 1 - upstream, one, 0)

    def finish(frame):
        span = parts.shape[2]
        total[:span] = own(frame, chip)

        @pl.when(chip > 0)
        def _():
            hop(0, frame, chip).wait_recv()
            total[:span] = total[:span] + lands[0, frame, chip].astype(F32)

        @pl.when(chip < chips - 1)
        def _():
            hop(1, frame, chip).wait_recv()
            total[:span] = total[:span] + lands[1, frame, chip].astype(F32)

        for lot in range(lots):
            ready[frame, lot] = total[lot * area : lot * area + CELLS].astype(BF16)
        for step in range(n_frames - 1):
            handing(step, frame, group).start()
        out[group * frame_dev + frame] = ready[frame, pl.ds(group * blk_dev, blk_dev)]

    convolve(0)
    pl.semaphore_wait(barrier, 1 + len(sides) + len(peers))

    def advance(turn, carry):
        @pl.when((turn > 0) & (turn < frame_dev))
        def _():
            convolve(turn)

        @pl.when(turn < frame_dev)
        def _():
            cut_all(turn)

            @pl.when(near == 0)
            def _():
                move(near_way, turn)

        late = turn - far

        @pl.when((late >= 0) & (late < frame_dev))
        def _():
            finish(late)
            move(far_way, late)

        soon = turn - near

        @pl.when((near > 0) & (soon >= 0) & (soon < frame_dev))
        def _():
            move(near_way, soon)

        return carry

    lax.fori_loop(0, frame_dev + chips - 1, advance, 0)
    for frame in range(frame_dev):

        def drain(dest, carry):
            pairing(frame, dest).wait_send()

            @pl.when(dest != chip)
            def _():
                hop(0, frame, dest).wait_send()

            return carry

        lax.fori_loop(0, chips, drain, 0)
        for step in range(n_frames - 1):
            handing(step, frame, (group + n_frames - step - 1) % n_frames).wait()


def rms_scale(values, gain):
    return values * lax.rsqrt(jnp.mean(values * values, axis=-1, keepdims=True) + 1e-06) * gain


def token_kernel(
    bundle, steps, patch, query, starts, w_corr, w_feat, time_embed, gain_attn, w_qkv, w_attn_out, gain_mlp,
    w_up, w_down, out, tokens, w_token, w_qkv_t, mixed, hidden,
):
    step = pl.program_id(0)
    frames, _, cells, chans = patch.shape
    width = w_feat.shape[1]
    head = width // HEADS
    span = GROUP * frames
    per_block = QBLK // (GROUP * bundle)
    units = w_up.shape[1]
    lump = 4 * chans
    down = 2

    @pl.when(step == 0)
    def _():
        w_token[:chans] = jnp.zeros((chans, width), BF16)
        w_token[: w_corr.shape[0]] = w_corr[...]
        w_token[chans:] = w_feat[...]
        w_qkv_t[...] = w_qkv[...].T

    @pl.when((step % per_block == 0) & (step < steps))
    def _():
        queries = query[...]
        blank = jnp.zeros((chans - cells, chans), BF16)
        for some in range(0, frames, 4):
            corrs = []
            for frame in range(some, some + 4):
                window = jnp.concatenate([patch[frame, 0], blank], axis=0)
                corr = lax.dot_general(
                    queries, window, (((1,), (1,)), ((), ())), preferred_element_type=F32
                ) * chans ** (-0.5)
                corrs.append(jnp.concatenate([corr.astype(BF16), queries], axis=1))
            made = jnp.dot(jnp.concatenate(corrs, axis=0), w_token[...], preferred_element_type=F32)
            for n in range(4):
                whole = made[n * QBLK : (n + 1) * QBLK] + time_embed[some + n : some + n + 1, :]
                for plane in range(width // chans):
                    tokens[plane, pl.ds(some + n, QBLK, stride=frames), :] = whole[
                        :, plane * chans : (plane + 1) * chans
                    ]

    key_at = lax.broadcasted_iota(jnp.int32, (span, span), 0)
    query_at = lax.broadcasted_iota(jnp.int32, (span, span), 1)

    def attention():
        first = (step % per_block) * (GROUP * bundle)
        lines = pl.ds(pl.multiple_of(first * frames, span), bundle * span)
        x = jnp.concatenate([tokens[plane, lines, :] for plane in range(width // chans)], axis=1)
        normed = rms_scale(x, gain_attn[...]).astype(BF16)
        qkv = lax.dot_general(
            w_qkv_t[...], normed, (((1,), (1,)), ((), ())), preferred_element_type=F32
        ).astype(BF16)
        same = (key_at // frames) == (query_at // frames)
        power = head ** (-0.5) * math.log2(math.e)
        start_rows = jnp.broadcast_to(starts[...].astype(F32)[None, :], (GROUP, QBLK)).astype(BF16)
        source = lax.broadcasted_iota(jnp.int32, (QBLK, span), 0)
        track = lax.broadcasted_iota(jnp.int32, (QBLK, span), 1) // frames
        nothing = jnp.zeros((head, span), BF16)
        yield
        heads, scored, weighed = {}, {}, {}

        def score_pair(g, h):
            at = slice(g * span, (g + 1) * span)
            one = qkv[h * head : (h + 1) * head, at]
            two = qkv[(h + 1) * head : (h + 2) * head, at]
            pair = jnp.concatenate(
                [jnp.concatenate([one, nothing], axis=1), jnp.concatenate([nothing, two], axis=1)], axis=0
            )
            scored[g, h] = lax.dot_general(
                qkv[width + h * head : width + (h + 2) * head, at],
                pair,
                (((0,), (0,)), ((), ())),
                preferred_element_type=F32,
            )

        def weigh_pair(g, h):
            if h == 0:
                pick = (source == track + (first + GROUP * g)).astype(BF16)
                start = jnp.dot(start_rows, pick, preferred_element_type=F32)[:1].astype(jnp.int32)
                valid = same & ((key_at % frames) >= start)
                masks[g] = jnp.concatenate([valid, valid], axis=1)
            score = jnp.where(masks[g], scored.pop((g, h)), -1e30)
            weight = jnp.exp2((score - jnp.max(score, axis=0, keepdims=True)) * power)
            weighed[g, h] = weight.astype(BF16), jnp.sum(weight, axis=0, keepdims=True)

        def value_pair(g, h):
            at = slice(g * span, (g + 1) * span)
            weight, sums = weighed.pop((g, h))
            both = jnp.dot(
                qkv[2 * width + h * head : 2 * width + (h + 2) * head, at], weight, preferred_element_type=F32
            )
            heads[g, h] = (both[:head, :span] / sums[:, :span]).astype(BF16)
            heads[g, h + 1] = (both[head:, span:] / sums[:, span:]).astype(BF16)

        masks = {}
        pairs = [(g, h) for g in range(bundle) for h in range(0, HEADS, 2)]
        lead = 2
        for n in range(len(pairs) + 2 * lead):
            if n < len(pairs):
                score_pair(*pairs[n])
            if 0 <= n - lead < len(pairs):
                weigh_pair(*pairs[n - lead])
            if 0 <= n - 2 * lead < len(pairs):
                value_pair(*pairs[n - 2 * lead])
            if n < len(pairs):
                yield
        gathered = [jnp.concatenate([heads[g, h] for h in range(HEADS)], axis=0) for g in range(bundle)]
        attended = jnp.concatenate(gathered, axis=1)
        mixed[step % 2] = x + lax.dot_general(
            attended, w_attn_out[...], (((0,), (0,)), ((), ())), preferred_element_type=F32
        )
        yield

    def feed_forward():
        base = mixed[(step + 1) % 2]
        normed2 = rms_scale(base, gain_mlp[...]).astype(BF16)
        yield
        for at in range(0, units, lump):
            hidden[:, at : at + lump] = jax.nn.gelu(
                jnp.dot(normed2, w_up[:, at : at + lump], preferred_element_type=F32), approximate=True
            ).astype(BF16)
            yield
        for part in range(down):
            stretch = bundle * span // down
            lines = slice(part * stretch, (part + 1) * stretch)
            out[lines, :] = (
                base[lines] + jnp.dot(hidden[lines, :], w_down[...], preferred_element_type=F32)
            ).astype(BF16)
            yield

    @pl.when(step == 0)
    def _():
        for _ in attention():
            pass

    @pl.when((step > 0) & (step < steps))
    def _():
        ahead, behind = attention(), feed_forward()
        next(behind)
        next(ahead)
        total = bundle * HEADS // 2
        parts = units // lump + down
        done = 0
        for n in range(total):
            next(ahead)
            while done < parts and (done + 1) * total <= (n + 1) * parts:
                next(behind)
                done += 1
        for rest in (ahead, behind):
            for _ in rest:
                pass

    @pl.when(step == steps)
    def _():
        for _ in feed_forward():
            pass


def grant(scratch):
    held = 0
    for ref in scratch:
        if getattr(ref, "memory_space", None) == pltpu.VMEM:
            held += math.prod(ref.shape) * jnp.dtype(ref.dtype).itemsize
    return min(held + 6 * 2**20, 58 * 2**20)


def body(
    features, w_conv, query_feats, offset_rows, offset_cols, owners, start_frames, w_corr, w_feat,
    time_embed, gain_attn, w_qkv, w_attn_out, gain_mlp, w_up, w_down,
):
    n_tiles = lax.axis_size("tiles")
    n_frames = lax.axis_size("frames")
    frame_dev, rows, cols, chans = features.shape
    blocks = owners.shape[0]
    blk_dev = blocks // (n_frames * n_tiles)
    lots = n_frames * blk_dev
    frames_total = frame_dev * n_frames
    width = w_feat.shape[1]
    whole = pl.BlockSpec(memory_space=pltpu.VMEM)

    chips = n_tiles // 2
    span_rows = -(-lots * WIN * WIN // 8) * 8
    total_rows = -(-((lots - 1) * WIN * WIN + CELLS) // 8) * 8
    scratch = [
        pltpu.SMEM((blocks,), jnp.int32),
        pltpu.SMEM((frame_dev, blocks), jnp.int32),
        pltpu.SMEM((frame_dev, blocks), jnp.int32),
        pltpu.VMEM(w_conv.shape, BF16),
        pltpu.VMEM((3 * chans, 3 * chans), BF16),
        pltpu.VMEM((frame_dev, rows + 4, cols, chans), BF16),
        pltpu.VMEM((rows + 2 + 2 * WIN, cols + 16, chans), F32),
        pltpu.VMEM((2, span_rows, chans), F32),
        pltpu.VMEM((frame_dev, n_tiles, span_rows, chans), BF16),
        pltpu.VMEM((frame_dev, chips, span_rows, chans), BF16),
        pltpu.VMEM((frame_dev, chips, span_rows, chans), BF16),
        pltpu.VMEM((2, frame_dev, chips, span_rows, chans), BF16),
        pltpu.VMEM((total_rows, chans), F32),
        pltpu.VMEM((frame_dev, lots, CELLS, chans), BF16),
        pltpu.SemaphoreType.DMA((4,)),
        pltpu.SemaphoreType.DMA((frame_dev,)),
        pltpu.SemaphoreType.DMA((frame_dev, chips)),
        pltpu.SemaphoreType.DMA((frame_dev, chips)),
        pltpu.SemaphoreType.DMA((frame_dev, chips)),
        pltpu.SemaphoreType.DMA((2, frame_dev, chips)),
        pltpu.SemaphoreType.DMA((n_frames - 1, frame_dev)),
        pltpu.SemaphoreType.DMA((n_frames - 1, frame_dev)),
    ]
    patch = pl.pallas_call(
        functools.partial(window_kernel, n_tiles, n_frames),
        out_shape=jax.ShapeDtypeStruct((frames_total, blk_dev, CELLS, chans), BF16),
        in_specs=[pl.BlockSpec(memory_space=pltpu.HBM)] * 5,
        out_specs=whole,
        scratch_shapes=scratch,
        compiler_params=pltpu.CompilerParams(
            collective_id=0, has_side_effects=True, vmem_limit_bytes=grant(scratch)
        ),
    )(
        *[
            pltpu.with_memory_space_constraint(x, pltpu.HBM)
            for x in (owners[:, 0], offset_rows, offset_cols, features, w_conv)
        ]
    )

    bundle = 4
    span = GROUP * frames_total
    tracks = blk_dev * QBLK
    per_block = QBLK // (GROUP * bundle)
    def fixed(shape):
        return pl.BlockSpec(shape, lambda s: (0,) * len(shape))

    steps = tracks // (GROUP * bundle)

    def block(s):
        return jnp.minimum(s, steps - 1) // per_block

    refined = pl.pallas_call(
        functools.partial(token_kernel, bundle, steps),
        grid=(steps + 1,),
        out_shape=jax.ShapeDtypeStruct((tracks * frames_total, width), BF16),
        in_specs=[
            pl.BlockSpec((frames_total, 1, CELLS, chans), lambda s: (0, block(s), 0, 0)),
            pl.BlockSpec((QBLK, chans), lambda s: (block(s), 0)),
            pl.BlockSpec((QBLK,), lambda s: (block(s),)),
            fixed(w_corr.shape),
            fixed(w_feat.shape),
            fixed(time_embed.shape),
            fixed((width,)),
            fixed(w_qkv.shape),
            fixed(w_attn_out.shape),
            fixed((width,)),
            fixed(w_up.shape),
            fixed(w_down.shape),
        ],
        out_specs=pl.BlockSpec((bundle * span, width), lambda s: (jnp.maximum(s - 1, 0), 0)),
        scratch_shapes=[
            pltpu.VMEM((width // chans, frames_total * QBLK, chans), F32),
            pltpu.VMEM((2 * chans, width), BF16),
            pltpu.VMEM((3 * width, width), BF16),
            pltpu.VMEM((2, bundle * span, width), F32),
            pltpu.VMEM((bundle * span, w_up.shape[1]), BF16),
        ],
        compiler_params=pltpu.CompilerParams(vmem_limit_bytes=30 * 2**20),
    )(
        patch, query_feats, start_frames, w_corr, w_feat, time_embed, gain_attn, w_qkv, w_attn_out, gain_mlp,
        w_up, w_down,
    )
    return refined.reshape(tracks, frames_total, width)


def solution(mesh):
    placed = (
        P("frames", "tiles", None, None),
        P(),
        P(("frames", "tiles"), None),
        P("frames", None),
        P("frames", None),
        P(),
        P(("frames", "tiles")),
    ) + (P(),) * 9
    return jax.shard_map(
        body,
        mesh=mesh,
        in_specs=placed,
        out_specs=P(("frames", "tiles"), None, None),
        check_vma=False,
    )
```

```python
import functools
import math

import jax
import jax.numpy as jnp
from jax import lax
from jax.experimental import pallas as pl
from jax.experimental.pallas import tpu as pltpu
from jax.sharding import PartitionSpec as P

HEADS = 8
WIN = 9
QBLK = 128
CELLS = 88
REACH = WIN // 2
GROUP = 8
F32 = jnp.float32
BF16 = jnp.bfloat16
MESH = pl.DeviceIdType.MESH


def window_kernel(
    n_tiles, n_frames, owners_in, row_in, col_in, feat, w_conv_in, query_in, w_corr_in, w_feat_in, time_in, gain_in,
    w_qkv_in, x_out, qkv_out, owners, row_off, col_off, w_conv, query, w_corr, w_token, time_embed, gain, w_qkv, w_cat,
    padded, conv, win, parts, pairs, sums, lands, total, ready, windows, load_sem, feat_sem, pair_send, pair_recv,
    hop_send, hop_recv, out_send, out_recv,
):
    tile, group = lax.axis_index("tiles"), lax.axis_index("frames")
    frame_dev, rows, cols, chans = feat.shape
    blocks = owners.shape[0]
    per_group = blocks // n_frames
    blk_dev = windows.shape[1]
    width = gain.shape[0]
    lots = n_frames * blk_dev
    area = WIN * WIN
    chips = n_tiles // 2
    chip, core = tile // 2, tile % 2
    first_half = 1 - (2 * chip) // chips
    near = (1 - first_half) * (chips - 1 - chip) + first_half * chip
    far = chips - 1 - near
    near_way, far_way = 1 - first_half, first_half

    def fetch(frame):
        return pltpu.make_async_copy(feat.at[frame], padded.at[frame, pl.ds(2, rows)], feat_sem.at[frame])

    loads = [
        pltpu.make_async_copy(source, target, load_sem.at[n])
        for n, (source, target) in enumerate(
            [
                (w_conv_in, w_conv), (owners_in, owners), (row_in, row_off), (col_in, col_off), (query_in, query),
                (w_corr_in, w_corr), (w_feat_in, w_token.at[pl.ds(chans, chans)]), (time_in, time_embed),
                (gain_in, gain), (w_qkv_in, w_qkv),
            ]
        )
    ]
    fetch(0).start()
    for load in loads:
        load.start()
    for frame in range(1, frame_dev):
        fetch(frame).start()
    partner = (group, tile + 1 - 2 * core)
    sides = [(group, (tile + 2) % n_tiles), (group, (tile + n_tiles - 2) % n_tiles)]
    peers = [((group + step) % n_frames, tile) for step in range(1, n_frames)]
    barrier = pltpu.get_barrier_semaphore()
    for device in [partner] + sides + peers:
        pl.semaphore_signal(barrier, inc=1, device_id=device, device_id_type=MESH)

    blank = jnp.zeros((2, cols, chans), BF16)
    for frame in range(frame_dev):
        padded[frame, 0:2] = blank
        padded[frame, rows + 2 : rows + 4] = blank
    win[...] = jnp.zeros_like(win)
    total[...] = jnp.zeros_like(total)
    for y in range(WIN):
        conv[y] = jnp.zeros(conv.shape[1:], F32)
        conv[WIN + rows + 2 + y] = jnp.zeros(conv.shape[1:], F32)
    conv[WIN : WIN + rows + 2, cols:] = jnp.zeros((rows + 2, conv.shape[1] - cols, chans), F32)
    for load in loads[:4]:
        load.wait()
    for a in range(3):
        for b in range(3):
            w_cat[a * chans : (a + 1) * chans, b * chans : (b + 1) * chans] = w_conv[a, b]

    def pairing(frame, dest):
        return pltpu.make_async_remote_copy(
            src_ref=parts.at[frame, 2 * dest + 1 - core],
            dst_ref=pairs.at[frame, dest],
            send_sem=pair_send.at[frame, dest],
            recv_sem=pair_recv.at[frame, dest],
            device_id=partner,
            device_id_type=MESH,
        )

    def hop(way, frame, dest):
        return pltpu.make_async_remote_copy(
            src_ref=sums.at[frame, dest],
            dst_ref=lands.at[way, frame, dest],
            send_sem=hop_send.at[frame, dest],
            recv_sem=hop_recv.at[way, frame, dest],
            device_id=(group, (tile + n_tiles + 2 - 4 * way) % n_tiles),
            device_id_type=MESH,
        )

    def handing(step, frame, giver):
        return pltpu.make_async_remote_copy(
            src_ref=ready.at[frame, pl.ds(peers[step][0] * blk_dev, blk_dev)],
            dst_ref=windows.at[giver * frame_dev + frame],
            send_sem=out_send.at[step, frame],
            recv_sem=out_recv.at[step, frame],
            device_id=peers[step],
            device_id_type=MESH,
        )

    def convolve(frame):
        fetch(frame).wait()

        def conv_rows(pair, carry):
            for half in range(2):
                y = 2 * pair + half
                wide = jnp.concatenate([padded[frame, y], padded[frame, y + 1], padded[frame, y + 2]], axis=-1)
                sums_at = jnp.dot(wide, w_cat[...], preferred_element_type=F32)
                edge = jnp.zeros((1, chans), F32)
                left = jnp.concatenate([edge, sums_at[: cols - 1, :chans]], axis=0)
                right = jnp.concatenate([sums_at[1:, 2 * chans :], edge], axis=0)
                conv[WIN + y, :cols] = left + sums_at[:, chans : 2 * chans] + right
            return carry

        lax.fori_loop(0, (rows + 2) // 2, conv_rows, 0)

        @pl.when(tile == 0)
        def _():
            conv[WIN, :cols] = jnp.zeros((cols, chans), F32)

        @pl.when(tile == n_tiles - 1)
        def _():
            conv[WIN + rows + 1, :cols] = jnp.zeros((cols, chans), F32)

    def cut_all(frame):
        def cut(turn, carry):
            dest = (1 - first_half) * turn + first_half * (chips - 1 - turn)
            for side in range(2):
                slot = 2 * dest + side
                for group_at in range(n_frames):
                    for extra in range(blk_dev):
                        block = group_at * per_group + slot * blk_dev + extra
                        local = (owners[block] - tile) * rows + row_off[frame, block] - REACH
                        first = jnp.clip(local + 1, -WIN, rows + 2) + WIN
                        col = col_off[frame, block]
                        at = (group_at * blk_dev + extra) * area
                        for i in range(WIN):
                            win[side, at + i * WIN : at + (i + 1) * WIN, :] = conv[first + i, pl.ds(col, WIN), :]
                parts[frame, slot] = win[side].astype(BF16)
            pairing(frame, dest).start()
            return carry

        lax.fori_loop(0, chips, cut, 0)

    def own(frame, dest):
        pairing(frame, dest).wait_recv()
        return parts[frame, 2 * dest + core].astype(F32) + pairs[frame, dest].astype(F32)

    def move(way, frame):
        upstream = (1 - way) * chip + way * (chips - 1 - chip)

        def one(i, carry):
            dest = (1 - way) * (chips - 1 - i) + way * i
            mine = own(frame, dest)

            @pl.when(upstream > 0)
            def _():
                hop(way, frame, dest).wait_recv()
                sums[frame, dest] = (mine + lands[way, frame, dest].astype(F32)).astype(BF16)

            @pl.when(upstream == 0)
            def _():
                sums[frame, dest] = mine.astype(BF16)

            hop(way, frame, dest).start()
            return carry

        lax.fori_loop(0, chips - 1 - upstream, one, 0)

    def finish(frame):
        span = parts.shape[2]
        total[:span] = own(frame, chip)

        @pl.when(chip > 0)
        def _():
            hop(0, frame, chip).wait_recv()
            total[:span] = total[:span] + lands[0, frame, chip].astype(F32)

        @pl.when(chip < chips - 1)
        def _():
            hop(1, frame, chip).wait_recv()
            total[:span] = total[:span] + lands[1, frame, chip].astype(F32)

        for lot in range(lots):
            ready[frame, lot] = total[lot * area : lot * area + CELLS].astype(BF16)
        for step in range(n_frames - 1):
            handing(step, frame, group).start()
        windows[group * frame_dev + frame] = ready[frame, pl.ds(group * blk_dev, blk_dev)]

    def project(frame):
        for step in range(n_frames - 1):
            handing(step, frame, (group + n_frames - step - 1) % n_frames).wait_recv()
        at_frames = [giver * frame_dev + frame for giver in range(n_frames)]
        blank = jnp.zeros((chans - CELLS, chans), BF16)
        per_blk = QBLK // GROUP
        for blk in range(blk_dev):
            queries = query[blk * QBLK : (blk + 1) * QBLK]
            corrs = []
            for at in at_frames:
                window = jnp.concatenate([windows[at, blk], blank], axis=0)
                corr = lax.dot_general(
                    queries, window, (((1,), (1,)), ((), ())), preferred_element_type=F32
                ) * chans ** (-0.5)
                corrs.append(jnp.concatenate([corr.astype(BF16), queries], axis=1))
            made = jnp.dot(jnp.concatenate(corrs, axis=0), w_token[...], preferred_element_type=F32)
            x = jnp.concatenate(
                [
                    made[n * QBLK : (n + 1) * QBLK] + time_embed[pl.ds(at, 1), :]
                    for n, at in enumerate(at_frames)
                ],
                axis=0,
            )
            normed = rms_scale(x, gain[...]).astype(BF16)
            qkv = jnp.dot(normed, w_qkv[...], preferred_element_type=F32).astype(BF16)
            for n, at in enumerate(at_frames):
                lines = pl.ds(pl.multiple_of(at * GROUP, GROUP), GROUP)
                held = slice(blk * per_blk, (blk + 1) * per_blk)
                x_out[held, lines, :] = x[n * QBLK : (n + 1) * QBLK].reshape(per_blk, GROUP, width)
                qkv_out[held, lines, :] = qkv[n * QBLK : (n + 1) * QBLK].reshape(per_blk, GROUP, 3 * width)

    convolve(0)
    for load in loads[4:]:
        load.wait()
    w_token[:chans] = jnp.zeros((chans, width), BF16)
    w_token[: w_corr.shape[0]] = w_corr[...]
    pl.semaphore_wait(barrier, 1 + len(sides) + len(peers))

    def advance(turn, carry):
        @pl.when((turn > 0) & (turn < frame_dev))
        def _():
            convolve(turn)

        @pl.when(turn < frame_dev)
        def _():
            cut_all(turn)

            @pl.when(near == 0)
            def _():
                move(near_way, turn)

        late = turn - far

        @pl.when((late >= 0) & (late < frame_dev))
        def _():
            move(far_way, late)

        @pl.when((late >= 1) & (late <= frame_dev))
        def _():
            project(late - 1)

        @pl.when((late >= 0) & (late < frame_dev))
        def _():
            finish(late)

        soon = turn - near

        @pl.when((near > 0) & (soon >= 0) & (soon < frame_dev))
        def _():
            move(near_way, soon)

        return carry

    lax.fori_loop(0, frame_dev + chips, advance, 0)
    for frame in range(frame_dev):

        def drain(dest, carry):
            pairing(frame, dest).wait_send()

            @pl.when(dest != chip)
            def _():
                hop(0, frame, dest).wait_send()

            return carry

        lax.fori_loop(0, chips, drain, 0)
        for step in range(n_frames - 1):
            handing(step, frame, group).wait_send()


def rms_scale(values, gain):
    return values * lax.rsqrt(jnp.mean(values * values, axis=-1, keepdims=True) + 1e-06) * gain


def token_kernel(
    bundle, steps, tokens, qkv, starts, w_attn_out, gain_mlp, w_up, w_down, out, mixed,
):
    step = pl.program_id(0)
    span, width = tokens.shape[1:]
    frames = span // GROUP
    chans = span
    head = width // HEADS
    per_block = QBLK // (GROUP * bundle)
    pieces = 3

    key_at = lax.broadcasted_iota(jnp.int32, (span, span), 0)
    query_at = lax.broadcasted_iota(jnp.int32, (span, span), 1)

    def attention():
        first = (step % per_block) * (GROUP * bundle)
        x = tokens[...].reshape(bundle * span, width)
        same = (key_at % GROUP) == (query_at % GROUP)
        power = head ** (-0.5) * math.log2(math.e)
        start_rows = jnp.broadcast_to(starts[...].astype(F32)[None, :], (GROUP, QBLK)).astype(BF16)
        source = lax.broadcasted_iota(jnp.int32, (QBLK, span), 0)
        track = lax.broadcasted_iota(jnp.int32, (QBLK, span), 1) % GROUP
        lane = lax.broadcasted_iota(jnp.int32, (span, width), 1) // head
        turned = {}
        yield
        heads, scored, weighed = {}, {}, {}

        def score_pair(g, h):
            if h == 0:
                turned[g] = qkv[g, :, 2 * width :].T
            low = h * head // chans * chans
            high = -(-(h + 2) * head // chans) * chans
            both = qkv[g, :, low:high]
            pair = jnp.concatenate(
                [jnp.where(lane[:, low:high] == h + n, both, jnp.zeros_like(both)) for n in range(2)], axis=0
            )
            scored[g, h] = lax.dot_general(
                qkv[g, :, width + low : width + high], pair, (((1,), (1,)), ((), ())), preferred_element_type=F32
            )

        def weigh_pair(g, h):
            if h == 0:
                pick = (source == track + (first + GROUP * g)).astype(BF16)
                start = jnp.dot(start_rows, pick, preferred_element_type=F32)[:1].astype(jnp.int32)
                valid = same & ((key_at // GROUP) >= start)
                masks[g] = jnp.concatenate([valid, valid], axis=1)
            score = jnp.where(masks[g], scored.pop((g, h)), -1e30)
            weight = jnp.exp2((score - jnp.max(score, axis=0, keepdims=True)) * power)
            weighed[g, h] = weight.astype(BF16), jnp.sum(weight, axis=0, keepdims=True)

        def value_pair(g, h):
            weight, sums = weighed.pop((g, h))
            both = jnp.dot(turned[g][h * head : (h + 2) * head], weight, preferred_element_type=F32)
            heads[g, h] = (both[:head, :span] / sums[:, :span]).astype(BF16)
            heads[g, h + 1] = (both[head:, span:] / sums[:, span:]).astype(BF16)

        masks = {}
        pairs = [(g, h) for g in range(bundle) for h in range(0, HEADS, 2)]
        lead = 2
        for n in range(len(pairs) + 2 * lead):
            if n < len(pairs):
                score_pair(*pairs[n])
            if 0 <= n - lead < len(pairs):
                weigh_pair(*pairs[n - lead])
            if 0 <= n - 2 * lead < len(pairs):
                value_pair(*pairs[n - 2 * lead])
            if n < len(pairs):
                yield
        gathered = [jnp.concatenate([heads[g, h] for h in range(HEADS)], axis=0) for g in range(bundle)]
        attended = jnp.concatenate(gathered, axis=1)
        mixed[step % 2] = x + lax.dot_general(
            attended, w_attn_out[...], (((0,), (0,)), ((), ())), preferred_element_type=F32
        )
        yield

    def feed_forward():
        move = (query_at == (key_at % frames) * GROUP + key_at // frames).astype(BF16)
        base = mixed[(step + 1) % 2]
        normed2 = rms_scale(base, gain_mlp[...]).astype(BF16)
        units = w_up.shape[1]
        lump = units // pieces
        result = base
        for piece in range(pieces):
            at = slice(piece * lump, (piece + 1) * lump)
            raised = jnp.dot(normed2, w_up[:, at], preferred_element_type=F32).astype(BF16)
            half = raised * 0.5
            inner = raised * (raised * raised * (0.044715 * math.sqrt(2 / math.pi)) + math.sqrt(2 / math.pi))
            result = result + jnp.dot(half + half * jnp.tanh(inner), w_down[at, :], preferred_element_type=F32)
            if piece + 1 < pieces:
                yield
        result = result.astype(BF16)
        for g in range(bundle):
            at = slice(g * span, (g + 1) * span)
            out[at, :] = jnp.dot(move, result[at, :], preferred_element_type=F32).astype(BF16)
        yield

    @pl.when(step == 0)
    def _():
        for _ in attention():
            pass

    @pl.when((step > 0) & (step < steps))
    def _():
        ahead, behind = attention(), feed_forward()
        next(ahead)
        total = bundle * HEADS // 2
        for n in range(total):
            next(ahead)
            if n in [total * piece // pieces for piece in range(pieces)]:
                next(behind)
        for rest in (ahead, behind):
            for _ in rest:
                pass

    @pl.when(step == steps)
    def _():
        for _ in feed_forward():
            pass


def grant(scratch):
    held = 0
    for ref in scratch:
        if getattr(ref, "memory_space", None) == pltpu.VMEM:
            held += math.prod(ref.shape) * jnp.dtype(ref.dtype).itemsize
    return min(held + 14 * 2**20, 62 * 2**20)


def body(
    features, w_conv, query_feats, offset_rows, offset_cols, owners, start_frames, w_corr, w_feat,
    time_embed, gain_attn, w_qkv, w_attn_out, gain_mlp, w_up, w_down,
):
    n_tiles = lax.axis_size("tiles")
    n_frames = lax.axis_size("frames")
    frame_dev, rows, cols, chans = features.shape
    blocks = owners.shape[0]
    blk_dev = blocks // (n_frames * n_tiles)
    lots = n_frames * blk_dev
    frames_total = frame_dev * n_frames
    width = w_feat.shape[1]
    whole = pl.BlockSpec(memory_space=pltpu.VMEM)

    chips = n_tiles // 2
    span_rows = -(-lots * WIN * WIN // 8) * 8
    total_rows = -(-((lots - 1) * WIN * WIN + CELLS) // 8) * 8
    scratch = [
        pltpu.SMEM((blocks,), jnp.int32),
        pltpu.SMEM((frame_dev, blocks), jnp.int32),
        pltpu.SMEM((frame_dev, blocks), jnp.int32),
        pltpu.VMEM(w_conv.shape, BF16),
        pltpu.VMEM(query_feats.shape, BF16),
        pltpu.VMEM(w_corr.shape, BF16),
        pltpu.VMEM((2 * chans, width), BF16),
        pltpu.VMEM(time_embed.shape, F32),
        pltpu.VMEM(gain_attn.shape, F32),
        pltpu.VMEM(w_qkv.shape, BF16),
        pltpu.VMEM((3 * chans, 3 * chans), BF16),
        pltpu.VMEM((frame_dev, rows + 4, cols, chans), BF16),
        pltpu.VMEM((rows + 2 + 2 * WIN, cols + 16, chans), F32),
        pltpu.VMEM((2, span_rows, chans), F32),
        pltpu.VMEM((frame_dev, n_tiles, span_rows, chans), BF16),
        pltpu.VMEM((frame_dev, chips, span_rows, chans), BF16),
        pltpu.VMEM((frame_dev, chips, span_rows, chans), BF16),
        pltpu.VMEM((2, frame_dev, chips, span_rows, chans), BF16),
        pltpu.VMEM((total_rows, chans), F32),
        pltpu.VMEM((frame_dev, lots, CELLS, chans), BF16),
        pltpu.VMEM((frames_total, blk_dev, CELLS, chans), BF16),
        pltpu.SemaphoreType.DMA((10,)),
        pltpu.SemaphoreType.DMA((frame_dev,)),
        pltpu.SemaphoreType.DMA((frame_dev, chips)),
        pltpu.SemaphoreType.DMA((frame_dev, chips)),
        pltpu.SemaphoreType.DMA((frame_dev, chips)),
        pltpu.SemaphoreType.DMA((2, frame_dev, chips)),
        pltpu.SemaphoreType.DMA((n_frames - 1, frame_dev)),
        pltpu.SemaphoreType.DMA((n_frames - 1, frame_dev)),
    ]
    tracks = blk_dev * QBLK
    span = GROUP * frames_total
    groups = tracks // GROUP
    given = (
        owners[:, 0], offset_rows, offset_cols, features, w_conv, query_feats, w_corr, w_feat, time_embed, gain_attn, w_qkv,
    )
    tokens, qkv = pl.pallas_call(
        functools.partial(window_kernel, n_tiles, n_frames),
        out_shape=[
            jax.ShapeDtypeStruct((groups, span, width), F32),
            jax.ShapeDtypeStruct((groups, span, 3 * width), BF16),
        ],
        in_specs=[pl.BlockSpec(memory_space=pltpu.HBM)] * len(given),
        out_specs=[whole, whole],
        scratch_shapes=scratch,
        compiler_params=pltpu.CompilerParams(
            collective_id=0, has_side_effects=True, vmem_limit_bytes=grant(scratch)
        ),
    )(*[pltpu.with_memory_space_constraint(x, pltpu.HBM) for x in given])

    bundle = 4
    per_block = QBLK // (GROUP * bundle)
    steps = groups // bundle

    def fixed(shape):
        return pl.BlockSpec(shape, lambda s: (0,) * len(shape))

    def ahead(s):
        return jnp.minimum(s, steps - 1)

    refined = pl.pallas_call(
        functools.partial(token_kernel, bundle, steps),
        grid=(steps + 1,),
        out_shape=jax.ShapeDtypeStruct((tracks * frames_total, width), BF16),
        in_specs=[
            pl.BlockSpec((bundle, span, width), lambda s: (ahead(s), 0, 0)),
            pl.BlockSpec((bundle, span, 3 * width), lambda s: (ahead(s), 0, 0)),
            pl.BlockSpec((QBLK,), lambda s: (ahead(s) // per_block,)),
            fixed(w_attn_out.shape),
            fixed((width,)),
            fixed(w_up.shape),
            fixed(w_down.shape),
        ],
        out_specs=pl.BlockSpec((bundle * span, width), lambda s: (jnp.maximum(s - 1, 0), 0)),
        scratch_shapes=[
            pltpu.VMEM((2, bundle * span, width), F32),
        ],
        compiler_params=pltpu.CompilerParams(vmem_limit_bytes=28 * 2**20),
    )(tokens, qkv, start_frames, w_attn_out, gain_mlp, w_up, w_down)
    return refined.reshape(tracks, frames_total, width)


def solution(mesh):
    placed = (
        P("frames", "tiles", None, None),
        P(),
        P(("frames", "tiles"), None),
        P("frames", None),
        P("frames", None),
        P(),
        P(("frames", "tiles")),
    ) + (P(),) * 9
    return jax.shard_map(
        body,
        mesh=mesh,
        in_specs=placed,
        out_specs=P(("frames", "tiles"), None, None),
        check_vma=False,
    )
```

```python
import functools
import math

import jax
import jax.numpy as jnp
from jax import lax
from jax.experimental import pallas as pl
from jax.experimental.pallas import tpu as pltpu
from jax.sharding import PartitionSpec as P

HEADS = 8
WIN = 9
QBLK = 128
CELLS = 88
REACH = WIN // 2
GROUP = 8
F32 = jnp.float32
BF16 = jnp.bfloat16
MESH = pl.DeviceIdType.MESH


def window_kernel(
    n_tiles, n_frames, owners_in, row_in, col_in, feat, w_conv_in, query_in, w_corr_in, w_feat_in, time_in, gain_in,
    w_qkv_in, x_out, qkv_out, owners, row_off, col_off, w_conv, query, w_corr, w_token, time_embed, gain, w_qkv, w_cat,
    padded, conv, win, parts, pairs, sums, lands, total, ready, windows, load_sem, feat_sem, pair_send, pair_recv,
    hop_send, hop_recv, out_send, out_recv,
):
    tile, group = lax.axis_index("tiles"), lax.axis_index("frames")
    frame_dev, rows, cols, chans = feat.shape
    blocks = owners.shape[0]
    per_group = blocks // n_frames
    blk_dev = windows.shape[1]
    width = gain.shape[0]
    lots = n_frames * blk_dev
    area = WIN * WIN
    chips = n_tiles // 2
    chip, core = tile // 2, tile % 2
    first_half = 1 - (2 * chip) // chips
    near = (1 - first_half) * (chips - 1 - chip) + first_half * chip
    far = chips - 1 - near
    near_way, far_way = 1 - first_half, first_half

    def fetch(frame):
        return pltpu.make_async_copy(feat.at[frame], padded.at[frame, pl.ds(2, rows)], feat_sem.at[frame])

    loads = [
        pltpu.make_async_copy(source, target, load_sem.at[n])
        for n, (source, target) in enumerate(
            [
                (w_conv_in, w_conv), (owners_in, owners), (row_in, row_off), (col_in, col_off), (query_in, query),
                (w_corr_in, w_corr), (w_feat_in, w_token.at[pl.ds(chans, chans)]), (time_in, time_embed),
                (gain_in, gain), (w_qkv_in, w_qkv),
            ]
        )
    ]
    fetch(0).start()
    for load in loads:
        load.start()
    for frame in range(1, frame_dev):
        fetch(frame).start()
    partner = (group, tile + 1 - 2 * core)
    sides = [(group, (tile + 2) % n_tiles), (group, (tile + n_tiles - 2) % n_tiles)]
    peers = [((group + step) % n_frames, tile) for step in range(1, n_frames)]
    barrier = pltpu.get_barrier_semaphore()
    for device in [partner] + sides + peers:
        pl.semaphore_signal(barrier, inc=1, device_id=device, device_id_type=MESH)

    blank = jnp.zeros((2, cols, chans), BF16)
    for frame in range(frame_dev):
        padded[frame, 0:2] = blank
        padded[frame, rows + 2 : rows + 4] = blank
    win[...] = jnp.zeros_like(win)
    total[...] = jnp.zeros_like(total)
    for y in range(WIN):
        conv[y] = jnp.zeros(conv.shape[1:], F32)
        conv[WIN + rows + 2 + y] = jnp.zeros(conv.shape[1:], F32)
    conv[WIN : WIN + rows + 2, cols:] = jnp.zeros((rows + 2, conv.shape[1] - cols, chans), F32)
    for load in loads[:4]:
        load.wait()
    for half in range(2):
        for b in range(3):
            at = (3 * half + b) * chans
            spare = 3 * (1 - half) * chans
            w_cat[spare : spare + chans, at : at + chans] = jnp.zeros((chans, chans), BF16)
            for a in range(3):
                w_cat[(half + a) * chans : (half + a + 1) * chans, at : at + chans] = w_conv[a, b]

    def pairing(frame, dest):
        return pltpu.make_async_remote_copy(
            src_ref=parts.at[frame, 2 * dest + 1 - core],
            dst_ref=pairs.at[frame, dest],
            send_sem=pair_send.at[frame, dest],
            recv_sem=pair_recv.at[frame, dest],
            device_id=partner,
            device_id_type=MESH,
        )

    def hop(way, frame, dest):
        return pltpu.make_async_remote_copy(
            src_ref=sums.at[frame, dest],
            dst_ref=lands.at[way, frame, dest],
            send_sem=hop_send.at[frame, dest],
            recv_sem=hop_recv.at[way, frame, dest],
            device_id=(group, (tile + n_tiles + 2 - 4 * way) % n_tiles),
            device_id_type=MESH,
        )

    def handing(step, frame, giver):
        return pltpu.make_async_remote_copy(
            src_ref=ready.at[frame, pl.ds(peers[step][0] * blk_dev, blk_dev)],
            dst_ref=windows.at[giver * frame_dev + frame],
            send_sem=out_send.at[step, frame],
            recv_sem=out_recv.at[step, frame],
            device_id=peers[step],
            device_id_type=MESH,
        )

    def convolve(frame):
        fetch(frame).wait()

        def conv_rows(pair, carry):
            y = 2 * pair
            wide = jnp.concatenate([padded[frame, y + n] for n in range(4)], axis=-1)
            made = jnp.dot(wide, w_cat[...], preferred_element_type=F32)
            edge = jnp.zeros((1, chans), F32)
            for half in range(2):
                at = 3 * half * chans
                left = jnp.concatenate([edge, made[: cols - 1, at : at + chans]], axis=0)
                right = jnp.concatenate([made[1:, at + 2 * chans : at + 3 * chans], edge], axis=0)
                conv[WIN + y + half, :cols] = left + made[:, at + chans : at + 2 * chans] + right
            return carry

        lax.fori_loop(0, (rows + 2) // 2, conv_rows, 0, unroll=True)

        @pl.when(tile == 0)
        def _():
            conv[WIN, :cols] = jnp.zeros((cols, chans), F32)

        @pl.when(tile == n_tiles - 1)
        def _():
            conv[WIN + rows + 1, :cols] = jnp.zeros((cols, chans), F32)

    def cut_all(frame):
        def cut(turn, carry):
            dest = (1 - first_half) * turn + first_half * (chips - 1 - turn)
            for side in range(2):
                slot = 2 * dest + side
                for group_at in range(n_frames):
                    for extra in range(blk_dev):
                        block = group_at * per_group + slot * blk_dev + extra
                        local = (owners[block] - tile) * rows + row_off[frame, block] - REACH
                        first = jnp.clip(local + 1, -WIN, rows + 2) + WIN
                        col = col_off[frame, block]
                        at = (group_at * blk_dev + extra) * area
                        for i in range(WIN):
                            win[side, at + i * WIN : at + (i + 1) * WIN, :] = conv[first + i, pl.ds(col, WIN), :]
                parts[frame, slot] = win[side].astype(BF16)
            pairing(frame, dest).start()
            return carry

        lax.fori_loop(0, chips, cut, 0)

    def own(frame, dest):
        pairing(frame, dest).wait_recv()
        return parts[frame, 2 * dest + core].astype(F32) + pairs[frame, dest].astype(F32)

    def move(way, frame):
        upstream = (1 - way) * chip + way * (chips - 1 - chip)

        def one(i, carry):
            dest = (1 - way) * (chips - 1 - i) + way * i
            mine = own(frame, dest)

            @pl.when(upstream > 0)
            def _():
                hop(way, frame, dest).wait_recv()
                sums[frame, dest] = (mine + lands[way, frame, dest].astype(F32)).astype(BF16)

            @pl.when(upstream == 0)
            def _():
                sums[frame, dest] = mine.astype(BF16)

            hop(way, frame, dest).start()
            return carry

        lax.fori_loop(0, chips - 1 - upstream, one, 0)

    def finish(frame):
        span = parts.shape[2]
        total[:span] = own(frame, chip)

        @pl.when(chip > 0)
        def _():
            hop(0, frame, chip).wait_recv()
            total[:span] = total[:span] + lands[0, frame, chip].astype(F32)

        @pl.when(chip < chips - 1)
        def _():
            hop(1, frame, chip).wait_recv()
            total[:span] = total[:span] + lands[1, frame, chip].astype(F32)

        for lot in range(lots):
            ready[frame, lot] = total[lot * area : lot * area + CELLS].astype(BF16)
        for step in range(n_frames - 1):
            handing(step, frame, group).start()
        windows[group * frame_dev + frame] = ready[frame, pl.ds(group * blk_dev, blk_dev)]

    def project(frame):
        for step in range(n_frames - 1):
            handing(step, frame, (group + n_frames - step - 1) % n_frames).wait_recv()
        at_frames = [giver * frame_dev + frame for giver in range(n_frames)]
        blank = jnp.zeros((chans - CELLS, chans), BF16)
        per_blk = QBLK // GROUP
        for blk in range(blk_dev):
            queries = query[blk * QBLK : (blk + 1) * QBLK]
            corrs = []
            for at in at_frames:
                window = jnp.concatenate([windows[at, blk], blank], axis=0)
                corr = lax.dot_general(
                    queries, window, (((1,), (1,)), ((), ())), preferred_element_type=F32
                ) * chans ** (-0.5)
                corrs.append(jnp.concatenate([corr.astype(BF16), queries], axis=1))
            made = jnp.dot(jnp.concatenate(corrs, axis=0), w_token[...], preferred_element_type=F32)
            x = jnp.concatenate(
                [
                    made[n * QBLK : (n + 1) * QBLK] + time_embed[pl.ds(at, 1), :]
                    for n, at in enumerate(at_frames)
                ],
                axis=0,
            )
            normed = rms_scale(x, gain[...]).astype(BF16)
            made = jnp.dot(normed, w_qkv[...], preferred_element_type=F32)
            power = (width // HEADS) ** (-0.5) * math.log2(math.e)
            qkv = jnp.concatenate([(made[:, :width] * power).astype(BF16), made[:, width:].astype(BF16)], axis=1)
            for n, at in enumerate(at_frames):
                lines = pl.ds(pl.multiple_of(at * GROUP, GROUP), GROUP)
                held = slice(blk * per_blk, (blk + 1) * per_blk)
                x_out[held, lines, :] = x[n * QBLK : (n + 1) * QBLK].reshape(per_blk, GROUP, width)
                qkv_out[held, lines, :] = qkv[n * QBLK : (n + 1) * QBLK].reshape(per_blk, GROUP, 3 * width)

    convolve(0)
    for load in loads[4:]:
        load.wait()
    w_token[:chans] = jnp.zeros((chans, width), BF16)
    w_token[: w_corr.shape[0]] = w_corr[...]
    pl.semaphore_wait(barrier, 1 + len(sides) + len(peers))

    def advance(turn, carry):
        @pl.when((turn > 0) & (turn < frame_dev))
        def _():
            convolve(turn)

        @pl.when(turn < frame_dev)
        def _():
            cut_all(turn)

            @pl.when(near == 0)
            def _():
                move(near_way, turn)

        late = turn - far

        @pl.when((late >= 0) & (late < frame_dev))
        def _():
            move(far_way, late)

        @pl.when((late >= 1) & (late <= frame_dev))
        def _():
            project(late - 1)

        @pl.when((late >= 0) & (late < frame_dev))
        def _():
            finish(late)

        soon = turn - near

        @pl.when((near > 0) & (soon >= 0) & (soon < frame_dev))
        def _():
            move(near_way, soon)

        return carry

    lax.fori_loop(0, frame_dev + chips, advance, 0)
    for frame in range(frame_dev):

        def drain(dest, carry):
            pairing(frame, dest).wait_send()

            @pl.when(dest != chip)
            def _():
                hop(0, frame, dest).wait_send()

            return carry

        lax.fori_loop(0, chips, drain, 0)
        for step in range(n_frames - 1):
            handing(step, frame, group).wait_send()


def rms_scale(values, gain):
    return values * lax.rsqrt(jnp.mean(values * values, axis=-1, keepdims=True) + 1e-06) * gain


def token_kernel(
    bundle, steps, tokens, qkv, starts, w_attn_out, gain_mlp, w_up, w_down, out, mixed,
):
    step = pl.program_id(0)
    span, width = tokens.shape[1:]
    frames = span // GROUP
    chans = span
    head = width // HEADS
    per_block = QBLK // (GROUP * bundle)
    pieces = 3

    key_at = lax.broadcasted_iota(jnp.int32, (span, span), 0)
    query_at = lax.broadcasted_iota(jnp.int32, (span, span), 1)

    def attention():
        first = (step % per_block) * (GROUP * bundle)
        x = tokens[...].reshape(bundle * span, width)
        same = (key_at % GROUP) == (query_at % GROUP)
        ones = jnp.ones((2 * GROUP, span), BF16)
        start_rows = jnp.broadcast_to(starts[...].astype(F32)[None, :], (GROUP, QBLK)).astype(BF16)
        source = lax.broadcasted_iota(jnp.int32, (QBLK, span), 0)
        track = lax.broadcasted_iota(jnp.int32, (QBLK, span), 1) % GROUP
        lane = lax.broadcasted_iota(jnp.int32, (span, width), 1) // head
        turned = {}
        yield
        heads, scored, weighed = {}, {}, {}

        def score_pair(g, h):
            if h == 0:
                turned[g] = qkv[g, :, 2 * width :].T
            low = h * head // chans * chans
            high = -(-(h + 2) * head // chans) * chans
            both = qkv[g, :, low:high]
            pair = jnp.concatenate(
                [jnp.where(lane[:, low:high] == h + n, both, jnp.zeros_like(both)) for n in range(2)], axis=0
            )
            scored[g, h] = lax.dot_general(
                qkv[g, :, width + low : width + high], pair, (((1,), (1,)), ((), ())), preferred_element_type=F32
            )

        def weigh_pair(g, h):
            if h == 0:
                pick = (source == track + (first + GROUP * g)).astype(BF16)
                start = jnp.dot(start_rows, pick, preferred_element_type=F32)[:1].astype(jnp.int32)
                valid = same & ((key_at // GROUP) >= start)
                masks[g] = jnp.concatenate([valid, valid], axis=1)
            score = jnp.where(masks[g], scored.pop((g, h)), -1e30)
            weighed[g, h] = jnp.exp2((score - jnp.max(score, axis=0, keepdims=True)).astype(BF16))

        def value_pair(g, h):
            lines = jnp.concatenate([turned[g][h * head : (h + 2) * head], ones], axis=0)
            both = jnp.dot(lines, weighed.pop((g, h)), preferred_element_type=F32)
            sums = 1.0 / both[2 * head : 2 * head + 1]
            heads[g, h] = (both[:head, :span] * sums[:, :span]).astype(BF16)
            heads[g, h + 1] = (both[head : 2 * head, span:] * sums[:, span:]).astype(BF16)

        masks = {}
        pairs = [(g, h) for g in range(bundle) for h in range(0, HEADS, 2)]
        lead = 4
        for n in range(len(pairs) + 2 * lead):
            if n < len(pairs):
                score_pair(*pairs[n])
            if 0 <= n - lead < len(pairs):
                weigh_pair(*pairs[n - lead])
            if 0 <= n - 2 * lead < len(pairs):
                value_pair(*pairs[n - 2 * lead])
            if n < len(pairs):
                yield
        gathered = [jnp.concatenate([heads[g, h] for h in range(HEADS)], axis=0) for g in range(bundle)]
        attended = jnp.concatenate(gathered, axis=1)
        mixed[step % 2] = x + lax.dot_general(
            attended, w_attn_out[...], (((0,), (0,)), ((), ())), preferred_element_type=F32
        )
        yield

    def feed_forward():
        move = (query_at == (key_at % frames) * GROUP + key_at // frames).astype(BF16)
        base = mixed[(step + 1) % 2]
        normed2 = rms_scale(base, gain_mlp[...]).astype(BF16)
        units = w_up.shape[1]
        lump = units // pieces
        result = base
        for piece in range(pieces):
            at = slice(piece * lump, (piece + 1) * lump)
            raised = jnp.dot(normed2, w_up[:, at], preferred_element_type=F32).astype(BF16)
            half = raised * 0.5
            inner = raised * (raised * raised * (0.044715 * math.sqrt(2 / math.pi)) + math.sqrt(2 / math.pi))
            result = result + jnp.dot(half + half * jnp.tanh(inner), w_down[at, :], preferred_element_type=F32)
            if piece + 1 < pieces:
                yield
        result = result.astype(BF16)
        for g in range(bundle):
            at = slice(g * span, (g + 1) * span)
            out[at, :] = jnp.dot(move, result[at, :], preferred_element_type=F32).astype(BF16)
        yield

    @pl.when(step == 0)
    def _():
        for _ in attention():
            pass

    @pl.when((step > 0) & (step < steps))
    def _():
        ahead, behind = attention(), feed_forward()
        next(ahead)
        total = bundle * HEADS // 2
        for n in range(total):
            next(ahead)
            if n in [total * piece // pieces for piece in range(pieces)]:
                next(behind)
        for rest in (ahead, behind):
            for _ in rest:
                pass

    @pl.when(step == steps)
    def _():
        for _ in feed_forward():
            pass


def grant(scratch):
    held = 0
    for ref in scratch:
        if getattr(ref, "memory_space", None) == pltpu.VMEM:
            held += math.prod(ref.shape) * jnp.dtype(ref.dtype).itemsize
    return min(held + 14 * 2**20, 62 * 2**20)


def body(
    features, w_conv, query_feats, offset_rows, offset_cols, owners, start_frames, w_corr, w_feat,
    time_embed, gain_attn, w_qkv, w_attn_out, gain_mlp, w_up, w_down,
):
    n_tiles = lax.axis_size("tiles")
    n_frames = lax.axis_size("frames")
    frame_dev, rows, cols, chans = features.shape
    blocks = owners.shape[0]
    blk_dev = blocks // (n_frames * n_tiles)
    lots = n_frames * blk_dev
    frames_total = frame_dev * n_frames
    width = w_feat.shape[1]
    whole = pl.BlockSpec(memory_space=pltpu.VMEM)

    chips = n_tiles // 2
    span_rows = -(-lots * WIN * WIN // 8) * 8
    total_rows = -(-((lots - 1) * WIN * WIN + CELLS) // 8) * 8
    scratch = [
        pltpu.SMEM((blocks,), jnp.int32),
        pltpu.SMEM((frame_dev, blocks), jnp.int32),
        pltpu.SMEM((frame_dev, blocks), jnp.int32),
        pltpu.VMEM(w_conv.shape, BF16),
        pltpu.VMEM(query_feats.shape, BF16),
        pltpu.VMEM(w_corr.shape, BF16),
        pltpu.VMEM((2 * chans, width), BF16),
        pltpu.VMEM(time_embed.shape, F32),
        pltpu.VMEM(gain_attn.shape, F32),
        pltpu.VMEM(w_qkv.shape, BF16),
        pltpu.VMEM((4 * chans, 6 * chans), BF16),
        pltpu.VMEM((frame_dev, rows + 4, cols, chans), BF16),
        pltpu.VMEM((rows + 2 + 2 * WIN, cols + 16, chans), F32),
        pltpu.VMEM((2, span_rows, chans), F32),
        pltpu.VMEM((frame_dev, n_tiles, span_rows, chans), BF16),
        pltpu.VMEM((frame_dev, chips, span_rows, chans), BF16),
        pltpu.VMEM((frame_dev, chips, span_rows, chans), BF16),
        pltpu.VMEM((2, frame_dev, chips, span_rows, chans), BF16),
        pltpu.VMEM((total_rows, chans), F32),
        pltpu.VMEM((frame_dev, lots, CELLS, chans), BF16),
        pltpu.VMEM((frames_total, blk_dev, CELLS, chans), BF16),
        pltpu.SemaphoreType.DMA((10,)),
        pltpu.SemaphoreType.DMA((frame_dev,)),
        pltpu.SemaphoreType.DMA((frame_dev, chips)),
        pltpu.SemaphoreType.DMA((frame_dev, chips)),
        pltpu.SemaphoreType.DMA((frame_dev, chips)),
        pltpu.SemaphoreType.DMA((2, frame_dev, chips)),
        pltpu.SemaphoreType.DMA((n_frames - 1, frame_dev)),
        pltpu.SemaphoreType.DMA((n_frames - 1, frame_dev)),
    ]
    tracks = blk_dev * QBLK
    span = GROUP * frames_total
    groups = tracks // GROUP
    given = (
        owners[:, 0], offset_rows, offset_cols, features, w_conv, query_feats, w_corr, w_feat, time_embed, gain_attn, w_qkv,
    )
    tokens, qkv = pl.pallas_call(
        functools.partial(window_kernel, n_tiles, n_frames),
        out_shape=[
            jax.ShapeDtypeStruct((groups, span, width), F32),
            jax.ShapeDtypeStruct((groups, span, 3 * width), BF16),
        ],
        in_specs=[pl.BlockSpec(memory_space=pltpu.HBM)] * len(given),
        out_specs=[whole, whole],
        scratch_shapes=scratch,
        compiler_params=pltpu.CompilerParams(
            collective_id=0, has_side_effects=True, vmem_limit_bytes=grant(scratch)
        ),
    )(*[pltpu.with_memory_space_constraint(x, pltpu.HBM) for x in given])

    bundle = 4
    per_block = QBLK // (GROUP * bundle)
    steps = groups // bundle

    def fixed(shape):
        return pl.BlockSpec(shape, lambda s: (0,) * len(shape))

    def ahead(s):
        return jnp.minimum(s, steps - 1)

    refined = pl.pallas_call(
        functools.partial(token_kernel, bundle, steps),
        grid=(steps + 1,),
        out_shape=jax.ShapeDtypeStruct((tracks * frames_total, width), BF16),
        in_specs=[
            pl.BlockSpec((bundle, span, width), lambda s: (ahead(s), 0, 0)),
            pl.BlockSpec((bundle, span, 3 * width), lambda s: (ahead(s), 0, 0)),
            pl.BlockSpec((QBLK,), lambda s: (ahead(s) // per_block,)),
            fixed(w_attn_out.shape),
            fixed((width,)),
            fixed(w_up.shape),
            fixed(w_down.shape),
        ],
        out_specs=pl.BlockSpec((bundle * span, width), lambda s: (jnp.maximum(s - 1, 0), 0)),
        scratch_shapes=[
            pltpu.VMEM((2, bundle * span, width), F32),
        ],
        compiler_params=pltpu.CompilerParams(vmem_limit_bytes=28 * 2**20),
    )(tokens, qkv, start_frames, w_attn_out, gain_mlp, w_up, w_down)
    return refined.reshape(tracks, frames_total, width)


def solution(mesh):
    placed = (
        P("frames", "tiles", None, None),
        P(),
        P(("frames", "tiles"), None),
        P("frames", None),
        P("frames", None),
        P(),
        P(("frames", "tiles")),
    ) + (P(),) * 9
    return jax.shard_map(
        body,
        mesh=mesh,
        in_specs=placed,
        out_specs=P(("frames", "tiles"), None, None),
        check_vma=False,
    )
```

```python
import functools
import math

import jax
import jax.numpy as jnp
from jax import lax
from jax.experimental import pallas as pl
from jax.experimental.pallas import tpu as pltpu
from jax.sharding import PartitionSpec as P

HEADS = 8
WIN = 9
QBLK = 128
CELLS = 88
REACH = WIN // 2
GROUP = 8
F32 = jnp.float32
BF16 = jnp.bfloat16
MESH = pl.DeviceIdType.MESH


def window_kernel(
    n_tiles, n_frames, owners_in, row_in, col_in, feat, w_conv_in, query_in, w_corr_in, w_feat_in, time_in, gain_in,
    w_qkv_in, x_out, qkv_out, owners, row_off, col_off, w_conv, query, w_corr, w_token, time_embed, gain, w_qkv, w_cat,
    padded, conv, win, parts, pairs, sums, lands, total, ready, windows, load_sem, feat_sem, pair_send, pair_recv,
    hop_send, hop_recv, out_send, out_recv,
):
    tile, group = lax.axis_index("tiles"), lax.axis_index("frames")
    frame_dev, rows, cols, chans = feat.shape
    blocks = owners.shape[0]
    per_group = blocks // n_frames
    blk_dev = windows.shape[1]
    width = gain.shape[0]
    lots = n_frames * blk_dev
    area = WIN * WIN
    chips = n_tiles // 2
    chip, core = tile // 2, tile % 2
    first_half = 1 - (2 * chip) // chips
    near = (1 - first_half) * (chips - 1 - chip) + first_half * chip
    far = chips - 1 - near
    near_way, far_way = 1 - first_half, first_half

    def fetch(frame):
        return pltpu.make_async_copy(feat.at[frame], padded.at[frame, pl.ds(2, rows)], feat_sem.at[frame])

    loads = [
        pltpu.make_async_copy(source, target, load_sem.at[n])
        for n, (source, target) in enumerate(
            [
                (w_conv_in, w_conv), (owners_in, owners), (row_in, row_off), (col_in, col_off), (query_in, query),
                (w_corr_in, w_corr), (w_feat_in, w_token.at[pl.ds(chans, chans)]), (time_in, time_embed),
                (gain_in, gain), (w_qkv_in, w_qkv),
            ]
        )
    ]
    fetch(0).start()
    for load in loads:
        load.start()
    for frame in range(1, frame_dev):
        fetch(frame).start()
    partner = (group, tile + 1 - 2 * core)
    sides = [(group, (tile + 2) % n_tiles), (group, (tile + n_tiles - 2) % n_tiles)]
    peers = [((group + step) % n_frames, tile) for step in range(1, n_frames)]
    barrier = pltpu.get_barrier_semaphore()
    for device in [partner] + sides + peers:
        pl.semaphore_signal(barrier, inc=1, device_id=device, device_id_type=MESH)

    blank = jnp.zeros((2, cols, chans), BF16)
    for frame in range(frame_dev):
        padded[frame, 0:2] = blank
        padded[frame, rows + 2 : rows + 4] = blank
    win[...] = jnp.zeros_like(win)
    total[...] = jnp.zeros_like(total)
    for y in range(WIN):
        conv[y] = jnp.zeros(conv.shape[1:], F32)
        conv[WIN + rows + 2 + y] = jnp.zeros(conv.shape[1:], F32)
    conv[WIN : WIN + rows + 2, cols:] = jnp.zeros((rows + 2, conv.shape[1] - cols, chans), F32)
    for load in loads[:4]:
        load.wait()
    for half in range(2):
        for b in range(3):
            at = (3 * half + b) * chans
            spare = 3 * (1 - half) * chans
            w_cat[spare : spare + chans, at : at + chans] = jnp.zeros((chans, chans), BF16)
            for a in range(3):
                w_cat[(half + a) * chans : (half + a + 1) * chans, at : at + chans] = w_conv[a, b]

    def pairing(frame, dest):
        return pltpu.make_async_remote_copy(
            src_ref=parts.at[frame, 2 * dest + 1 - core],
            dst_ref=pairs.at[frame, dest],
            send_sem=pair_send.at[frame, dest],
            recv_sem=pair_recv.at[frame, dest],
            device_id=partner,
            device_id_type=MESH,
        )

    def hop(way, frame, dest):
        return pltpu.make_async_remote_copy(
            src_ref=sums.at[frame, dest],
            dst_ref=lands.at[way, frame, dest],
            send_sem=hop_send.at[frame, dest],
            recv_sem=hop_recv.at[way, frame, dest],
            device_id=(group, (tile + n_tiles + 2 - 4 * way) % n_tiles),
            device_id_type=MESH,
        )

    def handing(step, frame, giver):
        return pltpu.make_async_remote_copy(
            src_ref=ready.at[frame, pl.ds(peers[step][0] * blk_dev, blk_dev)],
            dst_ref=windows.at[giver * frame_dev + frame],
            send_sem=out_send.at[step, frame],
            recv_sem=out_recv.at[step, frame],
            device_id=peers[step],
            device_id_type=MESH,
        )

    def convolve(frame):
        fetch(frame).wait()

        def conv_rows(pair, carry):
            y = 2 * pair
            wide = jnp.concatenate([padded[frame, y + n] for n in range(4)], axis=-1)
            made = jnp.dot(wide, w_cat[...], preferred_element_type=F32)
            edge = jnp.zeros((1, chans), F32)
            for half in range(2):
                at = 3 * half * chans
                left = jnp.concatenate([edge, made[: cols - 1, at : at + chans]], axis=0)
                right = jnp.concatenate([made[1:, at + 2 * chans : at + 3 * chans], edge], axis=0)
                conv[WIN + y + half, :cols] = left + made[:, at + chans : at + 2 * chans] + right
            return carry

        lax.fori_loop(0, (rows + 2) // 2, conv_rows, 0, unroll=True)

        @pl.when(tile == 0)
        def _():
            conv[WIN, :cols] = jnp.zeros((cols, chans), F32)

        @pl.when(tile == n_tiles - 1)
        def _():
            conv[WIN + rows + 1, :cols] = jnp.zeros((cols, chans), F32)

    def cut_all(frame):
        def cut(turn, carry):
            dest = (1 - first_half) * turn + first_half * (chips - 1 - turn)
            for side in range(2):
                slot = 2 * dest + side
                for group_at in range(n_frames):
                    for extra in range(blk_dev):
                        block = group_at * per_group + slot * blk_dev + extra
                        local = (owners[block] - tile) * rows + row_off[frame, block] - REACH
                        first = jnp.clip(local + 1, -WIN, rows + 2) + WIN
                        col = col_off[frame, block]
                        at = (group_at * blk_dev + extra) * area
                        for i in range(WIN):
                            win[side, at + i * WIN : at + (i + 1) * WIN, :] = conv[first + i, pl.ds(col, WIN), :]
                parts[frame, slot] = win[side].astype(BF16)
            pairing(frame, dest).start()
            return carry

        lax.fori_loop(0, chips, cut, 0)

    def own(frame, dest):
        pairing(frame, dest).wait_recv()
        return parts[frame, 2 * dest + core].astype(F32) + pairs[frame, dest].astype(F32)

    def move(way, frame):
        upstream = (1 - way) * chip + way * (chips - 1 - chip)

        def one(i, carry):
            dest = (1 - way) * (chips - 1 - i) + way * i
            mine = own(frame, dest)

            @pl.when(upstream > 0)
            def _():
                hop(way, frame, dest).wait_recv()
                sums[frame, dest] = (mine + lands[way, frame, dest].astype(F32)).astype(BF16)

            @pl.when(upstream == 0)
            def _():
                sums[frame, dest] = mine.astype(BF16)

            hop(way, frame, dest).start()
            return carry

        lax.fori_loop(0, chips - 1 - upstream, one, 0)

    def finish(frame):
        span = parts.shape[2]
        total[:span] = own(frame, chip)

        @pl.when(chip > 0)
        def _():
            hop(0, frame, chip).wait_recv()
            total[:span] = total[:span] + lands[0, frame, chip].astype(F32)

        @pl.when(chip < chips - 1)
        def _():
            hop(1, frame, chip).wait_recv()
            total[:span] = total[:span] + lands[1, frame, chip].astype(F32)

        for lot in range(lots):
            ready[frame, lot] = total[lot * area : lot * area + CELLS].astype(BF16)
        for step in range(n_frames - 1):
            handing(step, frame, group).start()
        windows[group * frame_dev + frame] = ready[frame, pl.ds(group * blk_dev, blk_dev)]

    def project(frame):
        for step in range(n_frames - 1):
            handing(step, frame, (group + n_frames - step - 1) % n_frames).wait_recv()
        at_frames = [giver * frame_dev + frame for giver in range(n_frames)]
        blank = jnp.zeros((chans - CELLS, chans), BF16)
        per_blk = QBLK // GROUP
        for blk in range(blk_dev):
            queries = query[blk * QBLK : (blk + 1) * QBLK]
            corrs = []
            for at in at_frames:
                window = jnp.concatenate([windows[at, blk], blank], axis=0)
                corr = lax.dot_general(
                    queries, window, (((1,), (1,)), ((), ())), preferred_element_type=F32
                ) * chans ** (-0.5)
                corrs.append(jnp.concatenate([corr.astype(BF16), queries], axis=1))
            made = jnp.dot(jnp.concatenate(corrs, axis=0), w_token[...], preferred_element_type=F32)
            x = jnp.concatenate(
                [
                    made[n * QBLK : (n + 1) * QBLK] + time_embed[pl.ds(at, 1), :]
                    for n, at in enumerate(at_frames)
                ],
                axis=0,
            )
            normed = rms_scale(x, gain[...]).astype(BF16)
            made = jnp.dot(normed, w_qkv[...], preferred_element_type=F32)
            power = (width // HEADS) ** (-0.5) * math.log2(math.e)
            qkv = jnp.concatenate([(made[:, :width] * power).astype(BF16), made[:, width:].astype(BF16)], axis=1)
            for n, at in enumerate(at_frames):
                lines = pl.ds(pl.multiple_of(at * GROUP, GROUP), GROUP)
                held = slice(blk * per_blk, (blk + 1) * per_blk)
                x_out[held, lines, :] = x[n * QBLK : (n + 1) * QBLK].reshape(per_blk, GROUP, width)
                qkv_out[held, lines, :] = qkv[n * QBLK : (n + 1) * QBLK].reshape(per_blk, GROUP, 3 * width)

    convolve(0)
    for load in loads[4:]:
        load.wait()
    w_token[:chans] = jnp.zeros((chans, width), BF16)
    w_token[: w_corr.shape[0]] = w_corr[...]
    pl.semaphore_wait(barrier, 1 + len(sides) + len(peers))

    def advance(turn, carry):
        @pl.when((turn > 0) & (turn < frame_dev))
        def _():
            convolve(turn)

        @pl.when(turn < frame_dev)
        def _():
            cut_all(turn)

            @pl.when(near == 0)
            def _():
                move(near_way, turn)

        late = turn - far

        @pl.when((late >= 0) & (late < frame_dev))
        def _():
            move(far_way, late)

        @pl.when((late >= 1) & (late <= frame_dev))
        def _():
            project(late - 1)

        @pl.when((late >= 0) & (late < frame_dev))
        def _():
            finish(late)

        soon = turn - near

        @pl.when((near > 0) & (soon >= 0) & (soon < frame_dev))
        def _():
            move(near_way, soon)

        return carry

    lax.fori_loop(0, frame_dev + chips, advance, 0)
    for frame in range(frame_dev):

        def drain(dest, carry):
            pairing(frame, dest).wait_send()

            @pl.when(dest != chip)
            def _():
                hop(0, frame, dest).wait_send()

            return carry

        lax.fori_loop(0, chips, drain, 0)
        for step in range(n_frames - 1):
            handing(step, frame, group).wait_send()


def rms_scale(values, gain):
    return values * lax.rsqrt(jnp.mean(values * values, axis=-1, keepdims=True) + 1e-06) * gain


def token_kernel(
    bundle, steps, tokens, qkv, starts, w_attn_out, gain_mlp, w_up, w_down, out, mixed,
):
    step = pl.program_id(0)
    span, width = tokens.shape[1:]
    frames = span // GROUP
    chans = span
    head = width // HEADS
    per_block = QBLK // (GROUP * bundle)
    pieces = 3

    key_at = lax.broadcasted_iota(jnp.int32, (span, span), 0)
    query_at = lax.broadcasted_iota(jnp.int32, (span, span), 1)

    def attention():
        first = (step % per_block) * (GROUP * bundle)
        x = tokens[...].reshape(bundle * span, width)
        same = (key_at % GROUP) == (query_at % GROUP)
        ones = jnp.ones((2 * GROUP, span), BF16)
        start_rows = jnp.broadcast_to(starts[...].astype(F32)[None, :], (GROUP, QBLK)).astype(BF16)
        source = lax.broadcasted_iota(jnp.int32, (QBLK, span), 0)
        track = lax.broadcasted_iota(jnp.int32, (QBLK, span), 1) % GROUP
        lane = lax.broadcasted_iota(jnp.int32, (span, width), 1) // head
        turned = {}
        yield
        heads, scored, weighed = {}, {}, {}

        def score_pair(g, h):
            if h == 0:
                turned[g] = qkv[g, :, 2 * width :].T
            low = h * head // chans * chans
            high = -(-(h + 2) * head // chans) * chans
            both = qkv[g, :, low:high]
            pair = jnp.concatenate(
                [jnp.where(lane[:, low:high] == h + n, both, jnp.zeros_like(both)) for n in range(2)], axis=0
            )
            scored[g, h] = lax.dot_general(
                qkv[g, :, width + low : width + high], pair, (((1,), (1,)), ((), ())), preferred_element_type=F32
            )

        def weigh_pair(g, h):
            if h == 0:
                pick = (source == track + (first + GROUP * g)).astype(BF16)
                start = jnp.dot(start_rows, pick, preferred_element_type=F32)[:1].astype(jnp.int32)
                valid = same & ((key_at // GROUP) >= start)
                masks[g] = jnp.concatenate([valid, valid], axis=1)
            score = jnp.where(masks[g], scored.pop((g, h)), -1e30)
            weighed[g, h] = jnp.exp2((score - jnp.max(score, axis=0, keepdims=True)).astype(BF16))

        def value_pair(g, h):
            lines = jnp.concatenate([turned[g][h * head : (h + 2) * head], ones], axis=0)
            both = jnp.dot(lines, weighed.pop((g, h)), preferred_element_type=F32)
            sums = 1.0 / both[2 * head : 2 * head + 1]
            heads[g, h] = (both[:head, :span] * sums[:, :span]).astype(BF16)
            heads[g, h + 1] = (both[head : 2 * head, span:] * sums[:, span:]).astype(BF16)

        masks = {}
        pairs = [(g, h) for g in range(bundle) for h in range(0, HEADS, 2)]
        lead = 6
        for n in range(len(pairs) + 2 * lead):
            if n < len(pairs):
                score_pair(*pairs[n])
            if 0 <= n - lead < len(pairs):
                weigh_pair(*pairs[n - lead])
            if 0 <= n - 2 * lead < len(pairs):
                value_pair(*pairs[n - 2 * lead])
            if n < len(pairs):
                yield
        gathered = [jnp.concatenate([heads[g, h] for h in range(HEADS)], axis=0) for g in range(bundle)]
        attended = jnp.concatenate(gathered, axis=1)
        mixed[step % 2] = x + lax.dot_general(
            attended, w_attn_out[...], (((0,), (0,)), ((), ())), preferred_element_type=F32
        )
        yield

    def feed_forward():
        move = (query_at == (key_at % frames) * GROUP + key_at // frames).astype(BF16)
        base = mixed[(step + 1) % 2]
        normed2 = rms_scale(base, gain_mlp[...]).astype(BF16)
        units = w_up.shape[1]
        lump = units // pieces
        result = base
        for piece in range(pieces):
            at = slice(piece * lump, (piece + 1) * lump)
            raised = jnp.dot(normed2, w_up[:, at], preferred_element_type=F32).astype(BF16)
            half = raised * 0.5
            inner = raised * (raised * raised * (0.044715 * math.sqrt(2 / math.pi)) + math.sqrt(2 / math.pi))
            result = result + jnp.dot(half + half * jnp.tanh(inner), w_down[at, :], preferred_element_type=F32)
            if piece + 1 < pieces:
                yield
        result = result.astype(BF16)
        for g in range(bundle):
            at = slice(g * span, (g + 1) * span)
            out[at, :] = jnp.dot(move, result[at, :], preferred_element_type=F32).astype(BF16)
        yield

    @pl.when(step == 0)
    def _():
        for _ in attention():
            pass

    @pl.when((step > 0) & (step < steps))
    def _():
        ahead, behind = attention(), feed_forward()
        next(ahead)
        total = bundle * HEADS // 2
        for n in range(total):
            next(ahead)
            if n in [total * piece // pieces for piece in range(pieces)]:
                next(behind)
        for rest in (ahead, behind):
            for _ in rest:
                pass

    @pl.when(step == steps)
    def _():
        for _ in feed_forward():
            pass


def grant(scratch):
    held = 0
    for ref in scratch:
        if getattr(ref, "memory_space", None) == pltpu.VMEM:
            held += math.prod(ref.shape) * jnp.dtype(ref.dtype).itemsize
    return min(held + 14 * 2**20, 62 * 2**20)


def body(
    features, w_conv, query_feats, offset_rows, offset_cols, owners, start_frames, w_corr, w_feat,
    time_embed, gain_attn, w_qkv, w_attn_out, gain_mlp, w_up, w_down,
):
    n_tiles = lax.axis_size("tiles")
    n_frames = lax.axis_size("frames")
    frame_dev, rows, cols, chans = features.shape
    blocks = owners.shape[0]
    blk_dev = blocks // (n_frames * n_tiles)
    lots = n_frames * blk_dev
    frames_total = frame_dev * n_frames
    width = w_feat.shape[1]
    whole = pl.BlockSpec(memory_space=pltpu.VMEM)

    chips = n_tiles // 2
    span_rows = -(-lots * WIN * WIN // 8) * 8
    total_rows = -(-((lots - 1) * WIN * WIN + CELLS) // 8) * 8
    scratch = [
        pltpu.SMEM((blocks,), jnp.int32),
        pltpu.SMEM((frame_dev, blocks), jnp.int32),
        pltpu.SMEM((frame_dev, blocks), jnp.int32),
        pltpu.VMEM(w_conv.shape, BF16),
        pltpu.VMEM(query_feats.shape, BF16),
        pltpu.VMEM(w_corr.shape, BF16),
        pltpu.VMEM((2 * chans, width), BF16),
        pltpu.VMEM(time_embed.shape, F32),
        pltpu.VMEM(gain_attn.shape, F32),
        pltpu.VMEM(w_qkv.shape, BF16),
        pltpu.VMEM((4 * chans, 6 * chans), BF16),
        pltpu.VMEM((frame_dev, rows + 4, cols, chans), BF16),
        pltpu.VMEM((rows + 2 + 2 * WIN, cols + 16, chans), F32),
        pltpu.VMEM((2, span_rows, chans), F32),
        pltpu.VMEM((frame_dev, n_tiles, span_rows, chans), BF16),
        pltpu.VMEM((frame_dev, chips, span_rows, chans), BF16),
        pltpu.VMEM((frame_dev, chips, span_rows, chans), BF16),
        pltpu.VMEM((2, frame_dev, chips, span_rows, chans), BF16),
        pltpu.VMEM((total_rows, chans), F32),
        pltpu.VMEM((frame_dev, lots, CELLS, chans), BF16),
        pltpu.VMEM((frames_total, blk_dev, CELLS, chans), BF16),
        pltpu.SemaphoreType.DMA((10,)),
        pltpu.SemaphoreType.DMA((frame_dev,)),
        pltpu.SemaphoreType.DMA((frame_dev, chips)),
        pltpu.SemaphoreType.DMA((frame_dev, chips)),
        pltpu.SemaphoreType.DMA((frame_dev, chips)),
        pltpu.SemaphoreType.DMA((2, frame_dev, chips)),
        pltpu.SemaphoreType.DMA((n_frames - 1, frame_dev)),
        pltpu.SemaphoreType.DMA((n_frames - 1, frame_dev)),
    ]
    tracks = blk_dev * QBLK
    span = GROUP * frames_total
    groups = tracks // GROUP
    given = (
        owners[:, 0], offset_rows, offset_cols, features, w_conv, query_feats, w_corr, w_feat, time_embed, gain_attn, w_qkv,
    )
    tokens, qkv = pl.pallas_call(
        functools.partial(window_kernel, n_tiles, n_frames),
        out_shape=[
            jax.ShapeDtypeStruct((groups, span, width), F32),
            jax.ShapeDtypeStruct((groups, span, 3 * width), BF16),
        ],
        in_specs=[pl.BlockSpec(memory_space=pltpu.HBM)] * len(given),
        out_specs=[whole, whole],
        scratch_shapes=scratch,
        compiler_params=pltpu.CompilerParams(
            collective_id=0, has_side_effects=True, vmem_limit_bytes=grant(scratch)
        ),
    )(*[pltpu.with_memory_space_constraint(x, pltpu.HBM) for x in given])

    bundle = 8
    per_block = QBLK // (GROUP * bundle)
    steps = groups // bundle

    def fixed(shape):
        return pl.BlockSpec(shape, lambda s: (0,) * len(shape))

    def ahead(s):
        return jnp.minimum(s, steps - 1)

    refined = pl.pallas_call(
        functools.partial(token_kernel, bundle, steps),
        grid=(steps + 1,),
        out_shape=jax.ShapeDtypeStruct((tracks * frames_total, width), BF16),
        in_specs=[
            pl.BlockSpec((bundle, span, width), lambda s: (ahead(s), 0, 0)),
            pl.BlockSpec((bundle, span, 3 * width), lambda s: (ahead(s), 0, 0)),
            pl.BlockSpec((QBLK,), lambda s: (ahead(s) // per_block,)),
            fixed(w_attn_out.shape),
            fixed((width,)),
            fixed(w_up.shape),
            fixed(w_down.shape),
        ],
        out_specs=pl.BlockSpec((bundle * span, width), lambda s: (jnp.maximum(s - 1, 0), 0)),
        scratch_shapes=[
            pltpu.VMEM((2, bundle * span, width), F32),
        ],
        compiler_params=pltpu.CompilerParams(vmem_limit_bytes=36 * 2**20),
    )(tokens, qkv, start_frames, w_attn_out, gain_mlp, w_up, w_down)
    return refined.reshape(tracks, frames_total, width)


def solution(mesh):
    placed = (
        P("frames", "tiles", None, None),
        P(),
        P(("frames", "tiles"), None),
        P("frames", None),
        P("frames", None),
        P(),
        P(("frames", "tiles")),
    ) + (P(),) * 9
    return jax.shard_map(
        body,
        mesh=mesh,
        in_specs=placed,
        out_specs=P(("frames", "tiles"), None, None),
        check_vma=False,
    )
```

```python
import functools
import math

import jax
import jax.numpy as jnp
from jax import lax
from jax.experimental import pallas as pl
from jax.experimental.pallas import tpu as pltpu
from jax.sharding import PartitionSpec as P

HEADS = 8
WIN = 9
QBLK = 128
CELLS = 88
REACH = WIN // 2
GROUP = 8
F32 = jnp.float32
BF16 = jnp.bfloat16
MESH = pl.DeviceIdType.MESH


def window_kernel(
    n_tiles, n_frames, owners_in, row_in, col_in, feat, w_conv_in, query_in, w_corr_in, w_feat_in, time_in, gain_in,
    w_qkv_in, x_out, qkv_out, owners, row_off, col_off, w_conv, query, w_corr, w_token, time_embed, gain, w_qkv, w_cat,
    padded, conv, win, parts, pairs, sums, lands, total, ready, windows, load_sem, feat_sem, pair_send, pair_recv,
    hop_send, hop_recv, out_send, out_recv,
):
    tile, group = lax.axis_index("tiles"), lax.axis_index("frames")
    frame_dev, rows, cols, chans = feat.shape
    blocks = owners.shape[0]
    per_group = blocks // n_frames
    blk_dev = windows.shape[1]
    width = gain.shape[0]
    lots = n_frames * blk_dev
    area = WIN * WIN
    chips = n_tiles // 2
    chip, core = tile // 2, tile % 2
    first_half = 1 - (2 * chip) // chips
    near = (1 - first_half) * (chips - 1 - chip) + first_half * chip
    far = chips - 1 - near
    near_way, far_way = 1 - first_half, first_half

    def fetch(frame):
        return pltpu.make_async_copy(feat.at[frame], padded.at[frame, pl.ds(2, rows)], feat_sem.at[frame])

    loads = [
        pltpu.make_async_copy(source, target, load_sem.at[n])
        for n, (source, target) in enumerate(
            [
                (w_conv_in, w_conv), (owners_in, owners), (row_in, row_off), (col_in, col_off), (query_in, query),
                (w_corr_in, w_corr), (w_feat_in, w_token.at[pl.ds(chans, chans)]), (time_in, time_embed),
                (gain_in, gain), (w_qkv_in, w_qkv),
            ]
        )
    ]
    fetch(0).start()
    for load in loads:
        load.start()
    for frame in range(1, frame_dev):
        fetch(frame).start()
    partner = (group, tile + 1 - 2 * core)
    sides = [(group, (tile + 2) % n_tiles), (group, (tile + n_tiles - 2) % n_tiles)]
    peers = [((group + step) % n_frames, tile) for step in range(1, n_frames)]
    barrier = pltpu.get_barrier_semaphore()
    for device in [partner] + sides + peers:
        pl.semaphore_signal(barrier, inc=1, device_id=device, device_id_type=MESH)

    blank = jnp.zeros((2, cols, chans), BF16)
    for frame in range(frame_dev):
        padded[frame, 0:2] = blank
        padded[frame, rows + 2 : rows + 4] = blank
    win[...] = jnp.zeros_like(win)
    total[...] = jnp.zeros_like(total)
    for y in range(WIN):
        conv[y] = jnp.zeros(conv.shape[1:], F32)
        conv[WIN + rows + 2 + y] = jnp.zeros(conv.shape[1:], F32)
    conv[WIN : WIN + rows + 2, cols:] = jnp.zeros((rows + 2, conv.shape[1] - cols, chans), F32)
    for load in loads[:4]:
        load.wait()
    for half in range(2):
        for b in range(3):
            at = (3 * half + b) * chans
            spare = 3 * (1 - half) * chans
            w_cat[spare : spare + chans, at : at + chans] = jnp.zeros((chans, chans), BF16)
            for a in range(3):
                w_cat[(half + a) * chans : (half + a + 1) * chans, at : at + chans] = w_conv[a, b]

    def pairing(frame, dest):
        return pltpu.make_async_remote_copy(
            src_ref=parts.at[frame, 2 * dest + 1 - core],
            dst_ref=pairs.at[frame, dest],
            send_sem=pair_send.at[frame, dest],
            recv_sem=pair_recv.at[frame, dest],
            device_id=partner,
            device_id_type=MESH,
        )

    def hop(way, frame, dest):
        return pltpu.make_async_remote_copy(
            src_ref=sums.at[frame, dest],
            dst_ref=lands.at[way, frame, dest],
            send_sem=hop_send.at[frame, dest],
            recv_sem=hop_recv.at[way, frame, dest],
            device_id=(group, (tile + n_tiles + 2 - 4 * way) % n_tiles),
            device_id_type=MESH,
        )

    def handing(step, frame, giver):
        return pltpu.make_async_remote_copy(
            src_ref=ready.at[frame, pl.ds(peers[step][0] * blk_dev, blk_dev)],
            dst_ref=windows.at[giver * frame_dev + frame],
            send_sem=out_send.at[step, frame],
            recv_sem=out_recv.at[step, frame],
            device_id=peers[step],
            device_id_type=MESH,
        )

    def convolve(frame):
        fetch(frame).wait()

        def conv_rows(pair, carry):
            y = 2 * pair
            wide = jnp.concatenate([padded[frame, y + n] for n in range(4)], axis=-1)
            made = jnp.dot(wide, w_cat[...], preferred_element_type=F32)
            edge = jnp.zeros((1, chans), F32)
            for half in range(2):
                at = 3 * half * chans
                left = jnp.concatenate([edge, made[: cols - 1, at : at + chans]], axis=0)
                right = jnp.concatenate([made[1:, at + 2 * chans : at + 3 * chans], edge], axis=0)
                conv[WIN + y + half, :cols] = left + made[:, at + chans : at + 2 * chans] + right
            return carry

        lax.fori_loop(0, (rows + 2) // 2, conv_rows, 0, unroll=True)

        @pl.when(tile == 0)
        def _():
            conv[WIN, :cols] = jnp.zeros((cols, chans), F32)

        @pl.when(tile == n_tiles - 1)
        def _():
            conv[WIN + rows + 1, :cols] = jnp.zeros((cols, chans), F32)

    def cut_all(frame):
        def cut(turn, carry):
            dest = (1 - first_half) * turn + first_half * (chips - 1 - turn)
            for side in range(2):
                slot = 2 * dest + side
                for group_at in range(n_frames):
                    for extra in range(blk_dev):
                        block = group_at * per_group + slot * blk_dev + extra
                        local = (owners[block] - tile) * rows + row_off[frame, block] - REACH
                        first = jnp.clip(local + 1, -WIN, rows + 2) + WIN
                        col = col_off[frame, block]
                        at = (group_at * blk_dev + extra) * area
                        for i in range(WIN):
                            win[side, at + i * WIN : at + (i + 1) * WIN, :] = conv[first + i, pl.ds(col, WIN), :]
                parts[frame, slot] = win[side].astype(BF16)
            pairing(frame, dest).start()
            return carry

        lax.fori_loop(0, chips, cut, 0)

    def own(frame, dest):
        pairing(frame, dest).wait_recv()
        return parts[frame, 2 * dest + core].astype(F32) + pairs[frame, dest].astype(F32)

    def move(way, frame):
        upstream = (1 - way) * chip + way * (chips - 1 - chip)

        def one(i, carry):
            dest = (1 - way) * (chips - 1 - i) + way * i
            mine = own(frame, dest)

            @pl.when(upstream > 0)
            def _():
                hop(way, frame, dest).wait_recv()
                sums[frame, dest] = (mine + lands[way, frame, dest].astype(F32)).astype(BF16)

            @pl.when(upstream == 0)
            def _():
                sums[frame, dest] = mine.astype(BF16)

            hop(way, frame, dest).start()
            return carry

        lax.fori_loop(0, chips - 1 - upstream, one, 0)

    def finish(frame):
        span = parts.shape[2]
        total[:span] = own(frame, chip)

        @pl.when(chip > 0)
        def _():
            hop(0, frame, chip).wait_recv()
            total[:span] = total[:span] + lands[0, frame, chip].astype(F32)

        @pl.when(chip < chips - 1)
        def _():
            hop(1, frame, chip).wait_recv()
            total[:span] = total[:span] + lands[1, frame, chip].astype(F32)

        for lot in range(lots):
            ready[frame, lot] = total[lot * area : lot * area + CELLS].astype(BF16)
        for step in range(n_frames - 1):
            handing(step, frame, group).start()
        windows[group * frame_dev + frame] = ready[frame, pl.ds(group * blk_dev, blk_dev)]

    def project(frame):
        for step in range(n_frames - 1):
            handing(step, frame, (group + n_frames - step - 1) % n_frames).wait_recv()
        at_frames = [giver * frame_dev + frame for giver in range(n_frames)]
        blank = jnp.zeros((chans - CELLS, chans), BF16)
        per_blk = QBLK // GROUP
        for blk in range(blk_dev):
            queries = query[blk * QBLK : (blk + 1) * QBLK]
            corrs = []
            for at in at_frames:
                window = jnp.concatenate([windows[at, blk], blank], axis=0)
                corr = lax.dot_general(
                    queries, window, (((1,), (1,)), ((), ())), preferred_element_type=F32
                ) * chans ** (-0.5)
                corrs.append(jnp.concatenate([corr.astype(BF16), queries], axis=1))
            made = jnp.dot(jnp.concatenate(corrs, axis=0), w_token[...], preferred_element_type=F32)
            x = jnp.concatenate(
                [
                    made[n * QBLK : (n + 1) * QBLK] + time_embed[pl.ds(at, 1), :]
                    for n, at in enumerate(at_frames)
                ],
                axis=0,
            )
            normed = rms_scale(x, gain[...]).astype(BF16)
            made = jnp.dot(normed, w_qkv[...], preferred_element_type=F32)
            power = (width // HEADS) ** (-0.5) * math.log2(math.e)
            qkv = jnp.concatenate([(made[:, :width] * power).astype(BF16), made[:, width:].astype(BF16)], axis=1)
            for n, at in enumerate(at_frames):
                lines = pl.ds(pl.multiple_of(at * GROUP, GROUP), GROUP)
                held = slice(blk * per_blk, (blk + 1) * per_blk)
                x_out[held, lines, :] = x[n * QBLK : (n + 1) * QBLK].reshape(per_blk, GROUP, width)
                qkv_out[held, lines, :] = qkv[n * QBLK : (n + 1) * QBLK].reshape(per_blk, GROUP, 3 * width)

    convolve(0)
    for load in loads[4:]:
        load.wait()
    w_token[:chans] = jnp.zeros((chans, width), BF16)
    w_token[: w_corr.shape[0]] = w_corr[...]
    pl.semaphore_wait(barrier, 1 + len(sides) + len(peers))

    def advance(turn, carry):
        @pl.when((turn > 0) & (turn < frame_dev))
        def _():
            convolve(turn)

        @pl.when(turn < frame_dev)
        def _():
            cut_all(turn)

            @pl.when(near == 0)
            def _():
                move(near_way, turn)

        late = turn - far

        @pl.when((late >= 0) & (late < frame_dev))
        def _():
            move(far_way, late)

        @pl.when((late >= 1) & (late <= frame_dev))
        def _():
            project(late - 1)

        @pl.when((late >= 0) & (late < frame_dev))
        def _():
            finish(late)

        soon = turn - near

        @pl.when((near > 0) & (soon >= 0) & (soon < frame_dev))
        def _():
            move(near_way, soon)

        return carry

    lax.fori_loop(0, frame_dev + chips, advance, 0)
    for frame in range(frame_dev):

        def drain(dest, carry):
            pairing(frame, dest).wait_send()

            @pl.when(dest != chip)
            def _():
                hop(0, frame, dest).wait_send()

            return carry

        lax.fori_loop(0, chips, drain, 0)
        for step in range(n_frames - 1):
            handing(step, frame, group).wait_send()


def rms_scale(values, gain):
    return values * lax.rsqrt(jnp.mean(values * values, axis=-1, keepdims=True) + 1e-06) * gain


def token_kernel(
    bundle, steps, tokens, qkv, starts, w_attn_out, gain_mlp, w_up, w_down, out, mixed,
):
    step = pl.program_id(0)
    span, width = tokens.shape[1:]
    frames = span // GROUP
    chans = span
    head = width // HEADS
    per_block = QBLK // (GROUP * bundle)
    pieces = 3

    key_at = lax.broadcasted_iota(jnp.int32, (span, span), 0)
    query_at = lax.broadcasted_iota(jnp.int32, (span, span), 1)

    def attention():
        first = (step % per_block) * (GROUP * bundle)
        x = tokens[...].reshape(bundle * span, width)
        same = (key_at % GROUP) == (query_at % GROUP)
        ones = jnp.ones((2 * GROUP, span), BF16)
        start_rows = jnp.broadcast_to(starts[...].astype(F32)[None, :], (GROUP, QBLK)).astype(BF16)
        source = lax.broadcasted_iota(jnp.int32, (QBLK, span), 0)
        track = lax.broadcasted_iota(jnp.int32, (QBLK, span), 1) % GROUP
        lane = lax.broadcasted_iota(jnp.int32, (span, width), 1) // head
        turned = {}
        yield
        heads, scored, weighed = {}, {}, {}

        def score_pair(g, h):
            if h == 0:
                turned[g] = qkv[g, :, 2 * width :].T
            low = h * head // chans * chans
            high = -(-(h + 2) * head // chans) * chans
            both = qkv[g, :, low:high]
            pair = jnp.concatenate(
                [jnp.where(lane[:, low:high] == h + n, both, jnp.zeros_like(both)) for n in range(2)], axis=0
            )
            scored[g, h] = lax.dot_general(
                qkv[g, :, width + low : width + high], pair, (((1,), (1,)), ((), ())), preferred_element_type=F32
            )

        def weigh_pair(g, h):
            if h == 0:
                pick = (source == track + (first + GROUP * g)).astype(BF16)
                start = jnp.dot(start_rows, pick, preferred_element_type=F32)[:1].astype(jnp.int32)
                valid = same & ((key_at // GROUP) >= start)
                masks[g] = jnp.concatenate([valid, valid], axis=1)
            score = jnp.where(masks[g], scored.pop((g, h)), -1e30)
            weighed[g, h] = jnp.exp2((score - jnp.max(score, axis=0, keepdims=True)).astype(BF16))

        def value_pair(g, h):
            lines = jnp.concatenate([turned[g][h * head : (h + 2) * head], ones], axis=0)
            both = jnp.dot(lines, weighed.pop((g, h)), preferred_element_type=F32)
            sums = 1.0 / both[2 * head : 2 * head + 1]
            heads[g, h] = (both[:head, :span] * sums[:, :span]).astype(BF16)
            heads[g, h + 1] = (both[head : 2 * head, span:] * sums[:, span:]).astype(BF16)

        masks = {}
        pairs = [(g, h) for g in range(bundle) for h in range(0, HEADS, 2)]
        lead = 6
        for n in range(len(pairs) + 2 * lead):
            if n < len(pairs):
                score_pair(*pairs[n])
            if 0 <= n - lead < len(pairs):
                weigh_pair(*pairs[n - lead])
            if 0 <= n - 2 * lead < len(pairs):
                value_pair(*pairs[n - 2 * lead])
            if n < len(pairs):
                yield
        gathered = [jnp.concatenate([heads[g, h] for h in range(HEADS)], axis=0) for g in range(bundle)]
        attended = jnp.concatenate(gathered, axis=1)
        mixed[step % 2] = x + lax.dot_general(
            attended, w_attn_out[...], (((0,), (0,)), ((), ())), preferred_element_type=F32
        )
        yield

    def feed_forward():
        move = (query_at == (key_at % frames) * GROUP + key_at // frames).astype(BF16)
        base = mixed[(step + 1) % 2]
        normed2 = rms_scale(base, gain_mlp[...]).astype(BF16)
        units = w_up.shape[1]
        lump = units // pieces
        result = base
        for piece in range(pieces):
            at = slice(piece * lump, (piece + 1) * lump)
            raised = jnp.dot(normed2, w_up[:, at], preferred_element_type=F32).astype(BF16)
            half = raised * 0.5
            inner = raised * (raised * raised * (0.044715 * math.sqrt(2 / math.pi)) + math.sqrt(2 / math.pi))
            result = result + jnp.dot(half + half * jnp.tanh(inner), w_down[at, :], preferred_element_type=F32)
            if piece + 1 < pieces:
                yield
        result = result.astype(BF16)
        for g in range(bundle):
            at = slice(g * span, (g + 1) * span)
            out[at, :] = jnp.dot(move, result[at, :], preferred_element_type=F32).astype(BF16)
        yield

    @pl.when(step == 0)
    def _():
        for _ in attention():
            pass

    @pl.when((step > 0) & (step < steps))
    def _():
        ahead, behind = attention(), feed_forward()
        next(ahead)
        total = bundle * HEADS // 2
        for n in range(total):
            next(ahead)
            if n in [total * (2 * piece + 1) // (2 * pieces) for piece in range(pieces)]:
                next(behind)
        for rest in (ahead, behind):
            for _ in rest:
                pass

    @pl.when(step == steps)
    def _():
        for _ in feed_forward():
            pass


def grant(scratch):
    held = 0
    for ref in scratch:
        if getattr(ref, "memory_space", None) == pltpu.VMEM:
            held += math.prod(ref.shape) * jnp.dtype(ref.dtype).itemsize
    return min(held + 14 * 2**20, 62 * 2**20)


def body(
    features, w_conv, query_feats, offset_rows, offset_cols, owners, start_frames, w_corr, w_feat,
    time_embed, gain_attn, w_qkv, w_attn_out, gain_mlp, w_up, w_down,
):
    n_tiles = lax.axis_size("tiles")
    n_frames = lax.axis_size("frames")
    frame_dev, rows, cols, chans = features.shape
    blocks = owners.shape[0]
    blk_dev = blocks // (n_frames * n_tiles)
    lots = n_frames * blk_dev
    frames_total = frame_dev * n_frames
    width = w_feat.shape[1]
    whole = pl.BlockSpec(memory_space=pltpu.VMEM)

    chips = n_tiles // 2
    span_rows = -(-lots * WIN * WIN // 8) * 8
    total_rows = -(-((lots - 1) * WIN * WIN + CELLS) // 8) * 8
    scratch = [
        pltpu.SMEM((blocks,), jnp.int32),
        pltpu.SMEM((frame_dev, blocks), jnp.int32),
        pltpu.SMEM((frame_dev, blocks), jnp.int32),
        pltpu.VMEM(w_conv.shape, BF16),
        pltpu.VMEM(query_feats.shape, BF16),
        pltpu.VMEM(w_corr.shape, BF16),
        pltpu.VMEM((2 * chans, width), BF16),
        pltpu.VMEM(time_embed.shape, F32),
        pltpu.VMEM(gain_attn.shape, F32),
        pltpu.VMEM(w_qkv.shape, BF16),
        pltpu.VMEM((4 * chans, 6 * chans), BF16),
        pltpu.VMEM((frame_dev, rows + 4, cols, chans), BF16),
        pltpu.VMEM((rows + 2 + 2 * WIN, cols + 16, chans), F32),
        pltpu.VMEM((2, span_rows, chans), F32),
        pltpu.VMEM((frame_dev, n_tiles, span_rows, chans), BF16),
        pltpu.VMEM((frame_dev, chips, span_rows, chans), BF16),
        pltpu.VMEM((frame_dev, chips, span_rows, chans), BF16),
        pltpu.VMEM((2, frame_dev, chips, span_rows, chans), BF16),
        pltpu.VMEM((total_rows, chans), F32),
        pltpu.VMEM((frame_dev, lots, CELLS, chans), BF16),
        pltpu.VMEM((frames_total, blk_dev, CELLS, chans), BF16),
        pltpu.SemaphoreType.DMA((10,)),
        pltpu.SemaphoreType.DMA((frame_dev,)),
        pltpu.SemaphoreType.DMA((frame_dev, chips)),
        pltpu.SemaphoreType.DMA((frame_dev, chips)),
        pltpu.SemaphoreType.DMA((frame_dev, chips)),
        pltpu.SemaphoreType.DMA((2, frame_dev, chips)),
        pltpu.SemaphoreType.DMA((n_frames - 1, frame_dev)),
        pltpu.SemaphoreType.DMA((n_frames - 1, frame_dev)),
    ]
    tracks = blk_dev * QBLK
    span = GROUP * frames_total
    groups = tracks // GROUP
    given = (
        owners[:, 0], offset_rows, offset_cols, features, w_conv, query_feats, w_corr, w_feat, time_embed, gain_attn, w_qkv,
    )
    tokens, qkv = pl.pallas_call(
        functools.partial(window_kernel, n_tiles, n_frames),
        out_shape=[
            jax.ShapeDtypeStruct((groups, span, width), F32),
            jax.ShapeDtypeStruct((groups, span, 3 * width), BF16),
        ],
        in_specs=[pl.BlockSpec(memory_space=pltpu.HBM)] * len(given),
        out_specs=[whole, whole],
        scratch_shapes=scratch,
        compiler_params=pltpu.CompilerParams(
            collective_id=0, has_side_effects=True, vmem_limit_bytes=grant(scratch)
        ),
    )(*[pltpu.with_memory_space_constraint(x, pltpu.HBM) for x in given])

    bundle = 8
    per_block = QBLK // (GROUP * bundle)
    steps = groups // bundle

    def fixed(shape):
        return pl.BlockSpec(shape, lambda s: (0,) * len(shape))

    def ahead(s):
        return jnp.minimum(s, steps - 1)

    refined = pl.pallas_call(
        functools.partial(token_kernel, bundle, steps),
        grid=(steps + 1,),
        out_shape=jax.ShapeDtypeStruct((tracks * frames_total, width), BF16),
        in_specs=[
            pl.BlockSpec((bundle, span, width), lambda s: (ahead(s), 0, 0)),
            pl.BlockSpec((bundle, span, 3 * width), lambda s: (ahead(s), 0, 0)),
            pl.BlockSpec((QBLK,), lambda s: (ahead(s) // per_block,)),
            fixed(w_attn_out.shape),
            fixed((width,)),
            fixed(w_up.shape),
            fixed(w_down.shape),
        ],
        out_specs=pl.BlockSpec((bundle * span, width), lambda s: (jnp.maximum(s - 1, 0), 0)),
        scratch_shapes=[
            pltpu.VMEM((2, bundle * span, width), F32),
        ],
        compiler_params=pltpu.CompilerParams(vmem_limit_bytes=36 * 2**20),
    )(tokens, qkv, start_frames, w_attn_out, gain_mlp, w_up, w_down)
    return refined.reshape(tracks, frames_total, width)


def solution(mesh):
    placed = (
        P("frames", "tiles", None, None),
        P(),
        P(("frames", "tiles"), None),
        P("frames", None),
        P("frames", None),
        P(),
        P(("frames", "tiles")),
    ) + (P(),) * 9
    return jax.shard_map(
        body,
        mesh=mesh,
        in_specs=placed,
        out_specs=P(("frames", "tiles"), None, None),
        check_vma=False,
    )
```
